256 devices in a mesh: slot: 16 (over y_hi, z), space: 16 (over y_lo, x, core).
Axes of the slice: x: 4, y: 4 (y_hi: 2, y_lo: 2; y = y_hi * 2 + y_lo), z: 8, core: 2. Of those that a mesh axis runs over, the one named last changes fastest.
Arguments:
- queries: bfloat16 [8192, 1024], P('space'), may hold values from -150 to 150
- raw_clip: bfloat16 [8, 32, 64, 2048], P(None, 'space', None, 'slot'), may hold values from -60 to 60
- pool_weight: bfloat16 [27, 2048], P(None, 'slot'), may hold values from -1.25 to 1.25
- old_memory: bfloat16 [16, 4, 16, 32, 2048], P('slot', None, 'space'), may hold values from -6 to 6
- valid_columns: int32 [17], replicated, may hold values from 16 to 32, as said below
- out_weight: bfloat16 [1024, 1024], replicated, may hold values from -0.1875 to 0.1875
Outputs:
- attended: bfloat16 [8192, 1024], P('space')
- fresh_memory: bfloat16 [4, 16, 32, 2048], P(None, 'space', None, 'slot')
- aged_memory: bfloat16 [16, 4, 16, 32, 2048], P('slot', None, 'space')
The draws below stay inside these ranges and needn't reach their ends.
Inputs may be any that keep to these rules, and one draw needn't show every extreme that they name: `valid_columns`: at least one entry equals 32.
All inputs are finite; a program needn't handle non-finite values.
Results may differ from the reference program's by a relative error of at most 0.0085.
Values may be sent and summed in bfloat16 or wider, within the bound.
A program may use at most 128 MiB of HBM per device.

```python
import jax
import jax.numpy as jnp
from jax import lax

D = 1024
H = 16
HD = 64
QDEV = 512
MF = 4
MC = 32
MR = 16
CF = 8
RR = 32
CC = 64
MTOK = 2048
QTOK = 8192
N_SLOT = 16


def draw_old_memory(key, part):
    shape_full = (N_SLOT, MF, MR, MC, 2 * D)
    sample = jax.random.normal(jax.random.fold_in(key, 101), shape_full, jnp.float32)
    return jnp.clip(sample, -6.0, 6.0).astype(jnp.bfloat16)


def draw_queries(key, part):
    sample = 2.5 * jax.random.normal(jax.random.fold_in(key, 111), (QTOK, D), jnp.float32)
    sample = jnp.clip(sample, -15.0, 15.0)
    return sample.astype(jnp.bfloat16)


def draw_raw_clip(key, part):
    shape_full = (CF, RR, CC, 2 * D)
    token_scale = jnp.exp(jax.random.uniform(jax.random.fold_in(key, 301), (CF, RR, CC, 1), jnp.float32, 0.0, jnp.log(10.0)))
    channel_scale = jnp.exp(jax.random.uniform(jax.random.fold_in(key, 302), (2 * D,), jnp.float32, jnp.log(0.1), 0.0))
    sample = jnp.clip(jax.random.normal(jax.random.fold_in(key, 303), shape_full, jnp.float32), -6.0, 6.0)
    return jnp.clip(sample * token_scale * channel_scale, -60.0, 60.0).astype(jnp.bfloat16)


def draw_valid_columns(key, part):
    counts = jax.random.randint(jax.random.fold_in(key, 401), (N_SLOT + 1,), MC // 2, MC + 1, jnp.int32)
    full_slot = jax.random.randint(jax.random.fold_in(key, 402), (), 0, N_SLOT + 1, jnp.int32)
    return counts.at[full_slot].set(MC)


def level_of(own_key, shape, split, least, top_value):
    loudness = 1.0
    for dim, parts in split:
        heights = jax.random.uniform(jax.random.fold_in(jax.random.fold_in(own_key, 6), dim), (parts,), jnp.float32, least / len(split), top_value / len(split))
        loudness = loudness * jnp.repeat(jnp.exp(heights), shape[dim] // parts).reshape((-1,) + (1,) * (len(shape) - 1 - dim))
    return loudness


def gaussian(stream_key, shape, width, bound, cuts=(), held_as=jnp.bfloat16):
    gain = level_of(stream_key, shape, cuts, -0.22, 0.18) if cuts else 1.0
    drawn = jax.random.normal(stream_key, shape, jnp.float32) * width * gain
    return jnp.minimum(jnp.maximum(drawn, -bound), bound).astype(held_as)


def setup_inputs(seed: int = 0) -> dict:
    splits = jax.random.split(jax.random.key(seed), 7)
    queries = draw_queries(jax.random.fold_in(splits[6], 71), 0)
    raw_clip = draw_raw_clip(jax.random.fold_in(splits[6], 71), 0)
    pool_weight = gaussian(splits[2], (27, 2 * D), 27 ** -0.5, 1.25, ((1, 16),))
    old_memory = draw_old_memory(jax.random.fold_in(splits[6], 71), 0)
    valid_columns = draw_valid_columns(jax.random.fold_in(splits[6], 71), 0)
    out_weight = gaussian(splits[5], (D, D), D ** -0.5, 0.1875)
    return dict(queries=queries, raw_clip=raw_clip, pool_weight=pool_weight, old_memory=old_memory, valid_columns=valid_columns, out_weight=out_weight)


def pool_clip(raw_clip, pool_weight):
    raw_values = raw_clip.astype(jnp.float32)
    padded = jnp.pad(raw_values, ((1, 0), (1, 0), (1, 0), (0, 0)))
    weight = pool_weight.astype(jnp.float32)
    pooled = jnp.zeros((MF, MR, MC, 2 * D), jnp.float32)
    for frame_tap in range(3):
        for row_tap in range(3):
            for column_tap in range(3):
                tapped = padded[frame_tap:frame_tap + 2 * MF:2, row_tap:row_tap + 2 * MR:2, column_tap:column_tap + 2 * MC:2]
                pooled = pooled + weight[9 * frame_tap + 3 * row_tap + column_tap] * tapped
    shaped = pooled.reshape(MF, MR, MC, H, 2, HD)
    center = lax.optimization_barrier(jnp.mean(shaped, axis=-1, keepdims=True))
    centered = shaped - center
    spread = lax.optimization_barrier(jnp.mean(centered * centered, axis=-1, keepdims=True))
    normed = centered * lax.rsqrt(spread + 1e-06)
    return normed.reshape(MF, MR, MC, 2 * D).astype(jnp.bfloat16)

def reference(queries, raw_clip, pool_weight, old_memory, valid_columns, out_weight):
    fresh_memory = pool_clip(raw_clip, pool_weight)
    memory = jnp.concatenate([fresh_memory.reshape(MTOK, H, 2, HD), old_memory.reshape(N_SLOT * MTOK, H, 2, HD)], axis=0)
    key_total = (N_SLOT + 1) * MTOK
    memory_heads = memory.transpose(1, 0, 2, 3)
    token_index = jnp.arange(key_total, dtype=jnp.int32)
    slot_index = (token_index // MTOK).astype(jnp.int32)
    column = token_index % MC
    usable = column < valid_columns[slot_index]
    query_heads = queries.reshape(QTOK, H, HD).transpose(1, 0, 2)

    def one_head(head_inputs):
        head_memory, head_queries = head_inputs
        key_rows = head_memory[:, 0, :]
        value_rows = head_memory[:, 1, :]

        def one_block(query_block):
            scores = jnp.dot(query_block, key_rows.T, preferred_element_type=jnp.float32) * HD ** (-0.5)
            scores = jnp.where(usable[None, :], scores, -1e+30)
            peak = lax.optimization_barrier(jnp.max(scores, axis=1, keepdims=True))
            weights = jnp.where(usable[None, :], jnp.exp(scores - peak), 0.0)
            weight_sum = lax.optimization_barrier(jnp.sum(weights, axis=1, keepdims=True))
            weighted = jnp.dot(weights.astype(jnp.bfloat16), value_rows, preferred_element_type=jnp.float32)
            return weighted / weight_sum
        blocks = lax.map(one_block, head_queries.reshape(QTOK // QDEV, QDEV, HD))
        return blocks.reshape(QTOK, HD)
    mixed_heads = lax.map(one_head, (memory_heads, query_heads))
    mixed = mixed_heads.transpose(1, 0, 2).reshape(QTOK, D).astype(jnp.bfloat16)
    attended = jnp.dot(mixed, out_weight, preferred_element_type=jnp.float32).astype(jnp.bfloat16)
    aged_memory = jnp.concatenate([jnp.zeros_like(old_memory[:1]), old_memory[:-1]], axis=0)
    return (attended, fresh_memory, aged_memory)
```

```python
import math

import jax
import jax.numpy as jnp
from jax import lax
from jax.experimental import pallas as pl
from jax.experimental.pallas import tpu as pltpu
from jax.sharding import PartitionSpec as P

F32 = jnp.float32
BF16 = jnp.bfloat16
MESH = pl.DeviceIdType.MESH
N = 16
HD = 64
TOK = 128
QB = 512
NK = (N + 1) * TOK
TQ = 256
MC = 32
MASKED = -1e30
PAIRS = N // 2
OWN = QB // N
RING = 8


def to(slot, space):
    return {"slot": slot, "space": space}


def remote(src, dst, send, recv, slot, space):
    return pltpu.make_async_remote_copy(
        src_ref=src, dst_ref=dst, send_sem=send, recv_sem=recv, device_id=to(slot, space), device_id_type=MESH
    )


def wait_bytes(ref, sem):
    pltpu.make_async_copy(ref, ref, sem).wait()


def kernel(
    q_hbm, raw_hbm, pw_ref, old_hbm, valid, w_hbm,
    out, fresh, aged,
    qv, qt, qall, kv, kaug, vt, S, qa, ot, lt, sb, rb, ls, lr, mx, mr, att, sel, wv, rawv, halo, xf, zeros,
    lsem, lsem2, lsem3, lsem4, lsem5,
    halo_s, halo_r, kv_s, kv_r, q_s, q_r, fr_s, fr_r, ag_s, ag_r, res_s, res_r, lse_s, lse_r, mx_s, mx_r, at_s, at_r,
):
    s = lax.axis_index("slot")
    p = lax.axis_index("space")
    lane = lambda shape: lax.broadcasted_iota(jnp.int32, shape, 1)

    q_copy = pltpu.make_async_copy(q_hbm, qv, lsem)
    q_copy.start()
    raw_copy = pltpu.make_async_copy(raw_hbm, rawv, lsem2)
    raw_copy.start()
    kv_copy = pltpu.make_async_copy(
        old_hbm.at[:, pl.ds(pl.multiple_of(p * TOK, TOK), TOK)], kv.at[p], lsem3
    )
    kv_copy.start()
    w_copy = pltpu.make_async_copy(w_hbm, wv, lsem4)
    w_copy.start()

    barrier = pltpu.get_barrier_semaphore()
    for d in range(1, N):
        pl.semaphore_signal(barrier, inc=1, device_id=to(s, lax.rem(p + d, N)), device_id_type=MESH)
    for d in range(1, N):
        pl.semaphore_signal(barrier, inc=1, device_id=to(lax.rem(s + d, N), p), device_id_type=MESH)

    @pl.when(s != p)
    def _():
        pl.semaphore_signal(barrier, inc=1, device_id=to(p, s), device_id_type=MESH)

    q_copy.wait()
    for c in range(PAIRS):
        qt[c * 128 : (c + 1) * 128, :] = qv[:, c * 128 : (c + 1) * 128].T

    row_i = lax.broadcasted_iota(jnp.int32, (256, N * HD), 0)
    col_i = lax.broadcasted_iota(jnp.int32, (256, N * HD), 1)
    sel[...] = jnp.where(row_i % 128 == col_i // HD, 1.0, 0.0).astype(BF16)
    ones_row = jnp.where(lax.broadcasted_iota(jnp.int32, (HD, TQ), 0) == 0, 1.0, 0.0).astype(BF16)
    for a in range(2):
        for t in range(4):
            qa[a, t, 3 * HD :, :] = ones_row

    @pl.when(s != p)
    def _():
        pl.semaphore_wait(barrier, 2 * (N - 1) + 1)

    @pl.when(s == p)
    def _():
        pl.semaphore_wait(barrier, 2 * (N - 1))

    @pl.when(p < N - 1)
    def _():
        remote(raw_hbm.at[:, 1], halo, halo_s, halo_r, s, p + 1).start()

    for d in range(1, N):
        peer = lax.rem(p + d, N)
        remote(
            old_hbm.at[:, pl.ds(pl.multiple_of(peer * TOK, TOK), TOK)], kv.at[p], kv_s, kv_r, s, peer
        ).start()
    for d in range(1, N):
        peer = lax.rem(p + d, N)
        remote(
            qt.at[pl.ds(pl.multiple_of(peer * HD, HD), HD), :], qall.at[p], q_s, q_r.at[p], s, peer
        ).start()

    @pl.when(s < N - 1)
    def _():
        remote(old_hbm, aged, ag_s, ag_r, s + 1, p).start()

    @pl.when(s == 0)
    def _():
        zeros[...] = jnp.zeros_like(zeros)
        pltpu.make_async_copy(zeros, aged, lsem5).start()

    raw_copy.wait()

    @pl.when(p > 0)
    def _():
        wait_bytes(halo, halo_r)

    @pl.when(p == 0)
    def _():
        halo[...] = jnp.zeros_like(halo)

    edge = jnp.zeros((8, 8, 128), F32)
    for b in range(3):
        xf[b, :, 0:8, :] = edge
        xf[b, :, 8:, :] = (halo[...] if b == 0 else rawv[:, b - 1]).astype(F32)
    weight = pw_ref[...].astype(F32)
    half = lane((MC, 128)) < HD
    for f in range(4):
        total = jnp.zeros((MC, 128), F32)
        for a in range(3):
            frame = 2 * f + a - 1
            if frame < 0:
                continue
            for b in range(3):
                for g in range(3):
                    tap = 9 * a + 3 * b + g
                    total += weight[tap : tap + 1, :] * xf[b, frame, pl.ds(7 + g, MC, stride=2), :]
        mean_lo = jnp.sum(jnp.where(half, total, 0.0), axis=1, keepdims=True) / HD
        mean_hi = jnp.sum(jnp.where(half, 0.0, total), axis=1, keepdims=True) / HD
        centred = total - jnp.where(half, mean_lo, mean_hi)
        square = centred * centred
        var_lo = jnp.sum(jnp.where(half, square, 0.0), axis=1, keepdims=True) / HD
        var_hi = jnp.sum(jnp.where(half, 0.0, square), axis=1, keepdims=True) / HD
        normed = centred * lax.rsqrt(jnp.where(half, var_lo, var_hi) + 1e-06)
        fresh[f * MC : (f + 1) * MC, :] = normed.astype(BF16)

    @pl.when(s != p)
    def _():
        remote(fresh, kv.at[N], fr_s, fr_r, p, s).start()

    @pl.when(s == p)
    def _():
        kv[N] = fresh[...]

    qall[p] = qt[pl.ds(pl.multiple_of(p * HD, HD), HD), :]

    def prepare(i, count):
        x = kv[i].astype(F32)
        turned = pltpu.roll(x, HD, 1)
        low = lane((TOK, TOK)) < HD
        column = lax.broadcasted_iota(jnp.int32, (TOK, TOK), 0) % MC
        mask = jnp.where((lane((TOK, TOK)) == HD) & (column >= count), MASKED, 0.0)
        row = pl.ds(pl.multiple_of(i * TOK, TOK), TOK)
        kaug[row, 0:128] = jnp.where(low, x, turned).astype(BF16)
        kaug[row, 128:256] = jnp.where(low, x, mask).astype(BF16)
        upper = lax.broadcasted_iota(jnp.int32, (TOK, TOK), 0) < HD
        vt[:, row] = jnp.where(upper, 1.0, x.T).astype(BF16)

    kv_copy.wait()
    wait_bytes(kv.at[pl.ds(0, N - 1)], kv_r)
    own_count = valid[s + 1]
    fresh_count = valid[0]

    def prepare_old(i, carry):
        prepare(i, own_count)
        return carry

    lax.fori_loop(0, N, prepare_old, 0)

    @pl.when(s != p)
    def _():
        wait_bytes(kv.at[N], fr_r)

    prepare(N, fresh_count)

    scale = HD ** (-0.5) * math.log2(math.e)
    pair0 = p // 2

    def pair_of(i):
        return lax.rem(pair0 - i + PAIRS, PAIRS)

    def build(i):
        pair = pair_of(i)
        a = i % 2
        for b in range(2):
            for h in range(2):
                x = qall[2 * pair + b, :, h * TQ : (h + 1) * TQ].astype(F32) * scale
                first = x.astype(BF16)
                x = x - first.astype(F32)
                second = x.astype(BF16)
                x = x - second.astype(F32)
                t = 2 * b + h
                qa[a, t, 0:HD, :] = first
                qa[a, t, HD : 2 * HD, :] = second
                qa[a, t, 2 * HD : 3 * HD, :] = x.astype(BF16)

    def scores(a, t, z):
        peak = None
        for c in range(0, NK, 128):
            block = jnp.dot(kaug[c : c + 128, :], qa[a, t], preferred_element_type=F32)
            S[z, c : c + 128, :] = block
            top = jnp.max(block.reshape(16, 8, TQ), axis=0)
            peak = top if peak is None else jnp.maximum(peak, top)
        return peak

    def weigh(pair, t, z, peak):
        top = jnp.max(peak, axis=0, keepdims=True)
        total = None
        for c in range(0, NK, 256):
            n = min(256, NK - c)
            weights = jnp.exp2(S[z, c : c + n, :] - top).astype(BF16)
            part = jnp.dot(vt[:, c : c + n], weights, preferred_element_type=F32)
            total = part if total is None else total + part
        b, h = t // 2, t % 2
        ot[b * HD : (b + 1) * HD, h * TQ : (h + 1) * TQ] = total[HD:, :] / total[:HD, :]
        lt[pl.ds(2 * pair + b, 1), h * TQ : (h + 1) * TQ] = top + jnp.log2(total[0:1, :])

    wait_bytes(qall.at[0], q_r.at[p + 1 - 2 * lax.rem(p, 2)])
    build(0)
    first_peak = scores(0, 0, 0)

    def step(i, peak):
        pair = pair_of(i)

        @pl.when(i < PAIRS - 1)
        def _():
            coming = pair_of(i + 1)
            wait_bytes(qall.at[0], q_r.at[2 * coming])
            wait_bytes(qall.at[0], q_r.at[2 * coming + 1])

        build(i + 1)
        for t in range(4):
            if t < 3:
                later = scores(i % 2, t + 1, (t + 1) % 2)
            else:
                later = scores((i + 1) % 2, 0, 0)
            weigh(pair, t, t % 2, peak)
            peak = later
        sb[pair] = ot[...].T.astype(BF16).reshape(N, OWN, 128)
        for d in range(1, N):
            owner = lax.rem(s + d, N)
            remote(sb.at[pair, owner], rb.at[s, pair], res_s, res_r, owner, p).start()
        return peak

    lax.fori_loop(0, PAIRS, step, first_peak)

    lse = lt[...]
    first = lse.astype(BF16).astype(F32)
    second = (lse - first).astype(BF16).astype(F32)
    third = lse - first - second
    stacked = jnp.concatenate([first, second, third, jnp.zeros((128 - 3 * N, QB), F32)], axis=0)
    ls[...] = stacked.T.astype(BF16).reshape(N, OWN, 128)
    for d in range(1, N):
        owner = lax.rem(s + d, N)
        remote(ls.at[owner], lr.at[s], lse_s, lse_r, owner, p).start()
    lr[s] = ls[s]
    rb[s] = sb[:, s]

    wait_bytes(lr.at[pl.ds(0, N - 1)], lse_r)
    parts = lr[...].astype(F32).reshape(N * OWN, 128)
    parts = parts + pltpu.roll(parts, 128 - N, 1) + pltpu.roll(parts, 128 - 2 * N, 1)
    parts = jnp.where(lane((N * OWN, 128)) < N, parts, 0.0).reshape(N, OWN, 128)
    share = jnp.exp2(parts - jnp.max(parts, axis=0, keepdims=True))
    share = (share / jnp.sum(share, axis=0, keepdims=True)).reshape(N * OWN, 128)
    share_hi = share.astype(BF16)
    share_lo = (share - share_hi.astype(F32)).astype(BF16)
    shares = jnp.concatenate([share_hi, share_lo], axis=1)
    wait_bytes(rb.at[pl.ds(0, N - 1)], res_r)
    for j in range(PAIRS):
        spread = jnp.dot(shares, sel[:, j * 128 : (j + 1) * 128], preferred_element_type=F32)
        mixed = jnp.sum(spread.reshape(N, OWN, 128) * rb[:, j].astype(F32), axis=0)
        mx[j] = mixed.astype(BF16)

    for d in range(1, N):
        peer = lax.rem(p + d, N)
        remote(mx.at[peer // 2], mr.at[p], mx_s, mx_r, s, peer).start()
    mr[p] = mx[p // 2]
    w_copy.wait()
    wait_bytes(mr.at[pl.ds(0, N - 1)], mx_r)
    odd = lax.rem(p, 2) == 1
    left = lane((OWN, 128)) < HD
    pieces = []
    for j in range(PAIRS):
        a = mr[2 * j].astype(F32)
        b = mr[2 * j + 1].astype(F32)
        a = jnp.where(odd, pltpu.roll(a, HD, 1), a)
        b = jnp.where(odd, b, pltpu.roll(b, HD, 1))
        pieces.append(jnp.where(left, a, b).astype(BF16))
    heads = jnp.concatenate(pieces, axis=1)
    att[...] = jnp.dot(heads, wv[...], preferred_element_type=F32).astype(BF16)

    y, z = s // RING, lax.rem(s, RING)

    def rows(index):
        return out.at[pl.ds(pl.multiple_of(index * OWN, OWN), OWN), :]

    def near(dz):
        return y * RING + lax.rem(z + dz + RING, RING)

    def far(dz):
        return (1 - y) * RING + lax.rem(z + dz + RING, RING)

    def give(index, target, src=None, count=0):
        remote(rows(index) if src is None else src, rows(index), at_s.at[count], at_r.at[index], target, p).start()

    def got(index):
        wait_bytes(rows(0), at_r.at[index])

    sent = [0]

    def push(index, target, src=None):
        give(index, target, src, sent[0])
        sent[0] += 1

    push(s, far(0), att)
    push(s, near(1), att)
    push(s, near(-1), att)
    out[pl.ds(pl.multiple_of(s * OWN, OWN), OWN), :] = att[...]
    got(far(0))
    push(far(0), near(1))
    push(far(0), near(-1))
    for k in range(1, 4):
        got(near(-k))
        push(near(-k), near(1))
        got(near(k))
        if k < 3:
            push(near(k), near(-1))
        got(far(-k))
        if k < 3:
            push(far(-k), near(1))
        got(far(k))
        push(far(k), near(-1))
    got(near(-4))
    got(far(4))

    for i in range(sent[0]):
        wait_bytes(rows(0), at_s.at[i])
    wait_bytes(kv.at[pl.ds(0, N - 1)], kv_s)
    wait_bytes(qall.at[pl.ds(0, N - 1)], q_s)
    wait_bytes(rb.at[pl.ds(0, N - 1)], res_s)
    wait_bytes(lr.at[pl.ds(0, N - 1)], lse_s)
    wait_bytes(mr.at[pl.ds(0, N - 1)], mx_s)

    @pl.when(p < N - 1)
    def _():
        wait_bytes(halo, halo_s)

    @pl.when(s != p)
    def _():
        wait_bytes(kv.at[N], fr_s)

    @pl.when(s < N - 1)
    def _():
        wait_bytes(old_hbm, ag_s)

    @pl.when(s > 0)
    def _():
        wait_bytes(old_hbm, ag_r)

    @pl.when(s == 0)
    def _():
        pltpu.make_async_copy(zeros, aged, lsem5).wait()


def local(queries, raw_clip, pool_weight, old_memory, valid_columns, out_weight):
    dma = pltpu.SemaphoreType.DMA
    anywhere = pl.BlockSpec(memory_space=pl.ANY)
    vmem = pl.BlockSpec(memory_space=pltpu.VMEM)
    attended, fresh, aged = pl.pallas_call(
        kernel,
        out_shape=(
            jax.ShapeDtypeStruct((QB, N * HD), BF16),
            jax.ShapeDtypeStruct((TOK, TOK), BF16),
            jax.ShapeDtypeStruct((TOK, N * TOK), BF16),
        ),
        in_specs=[anywhere, anywhere, vmem, anywhere, pl.BlockSpec(memory_space=pltpu.SMEM), anywhere],
        out_specs=(vmem, vmem, anywhere),
        scratch_shapes=[
            pltpu.VMEM((QB, N * HD), BF16),
            pltpu.VMEM((N * HD, QB), BF16),
            pltpu.VMEM((N, HD, QB), BF16),
            pltpu.VMEM((N + 1, TOK, TOK), BF16),
            pltpu.VMEM((NK, 256), BF16),
            pltpu.VMEM((128, NK), BF16),
            pltpu.VMEM((2, NK, TQ), F32),
            pltpu.VMEM((2, 4, 256, TQ), BF16),
            pltpu.VMEM((128, QB), F32),
            pltpu.VMEM((N, QB), F32),
            pltpu.VMEM((PAIRS, N, OWN, 128), BF16),
            pltpu.VMEM((N, PAIRS, OWN, 128), BF16),
            pltpu.VMEM((N, OWN, 128), BF16),
            pltpu.VMEM((N, OWN, 128), BF16),
            pltpu.VMEM((PAIRS, OWN, 128), BF16),
            pltpu.VMEM((N, OWN, 128), BF16),
            pltpu.VMEM((OWN, N * HD), BF16),
            pltpu.VMEM((256, N * HD), BF16),
            pltpu.VMEM((N * HD, N * HD), BF16),
            pltpu.VMEM((8, 2, 64, 128), BF16),
            pltpu.VMEM((8, 64, 128), BF16),
            pltpu.VMEM((3, 8, 72, 128), F32),
            pltpu.VMEM((TOK, N * TOK), BF16),
            dma, dma, dma, dma, dma,
            dma, dma, dma, dma, dma, dma((N,)), dma, dma, dma, dma, dma, dma, dma, dma, dma, dma, dma((16,)), dma((N,)),
        ],
        compiler_params=pltpu.CompilerParams(
            collective_id=0, has_side_effects=True, vmem_limit_bytes=48 << 20
        ),
        name="attend",
    )(
        queries,
        raw_clip,
        pool_weight,
        old_memory.reshape(TOK, N * TOK),
        valid_columns,
        out_weight,
    )
    return (attended, fresh.reshape(4, 1, MC, TOK), aged.reshape(old_memory.shape))


def solution(mesh):
    return jax.shard_map(
        local,
        mesh=mesh,
        in_specs=(
            P("space", None),
            P(None, "space", None, "slot"),
            P(None, "slot"),
            P("slot", None, "space", None, None),
            P(),
            P(),
        ),
        out_specs=(
            P("space", None),
            P(None, "space", None, "slot"),
            P("slot", None, "space", None, None),
        ),
        check_vma=False,
    )
```

```python
import math

import jax
import jax.numpy as jnp
from jax import lax
from jax.experimental import pallas as pl
from jax.experimental.pallas import tpu as pltpu
from jax.sharding import PartitionSpec as P

F32 = jnp.float32
BF16 = jnp.bfloat16
MESH = pl.DeviceIdType.MESH
N = 16
HD = 64
TOK = 128
QB = 512
NK = (N + 1) * TOK
TQ = 256
MC = 32
MASKED = -1e30
PAIRS = N // 2
OWN = QB // N
RING = 8
CUT = 2


def to(slot, space):
    return {"slot": slot, "space": space}


def remote(src, dst, send, recv, slot, space):
    return pltpu.make_async_remote_copy(
        src_ref=src, dst_ref=dst, send_sem=send, recv_sem=recv, device_id=to(slot, space), device_id_type=MESH
    )


def wait_bytes(ref, sem):
    pltpu.make_async_copy(ref, ref, sem).wait()


def kernel(
    q_hbm, raw_hbm, pw_ref, old_hbm, valid, w_hbm,
    out, fresh, aged,
    qv, qt, qall, kv, kaug, vt, S, qa, st, sm, ot, lt, sb, rb, ls, lr, mx, mr, att, sel, wv, rawv, halo, xf, zeros,
    lsem, lsem2, lsem3, lsem4, lsem5,
    halo_s, halo_r, kv_s, kv_r, kx_s, kx_r, q_s, q_r, fr_s, fr_r, fx_s, fx_r, ag_s, ag_r,
    res_s, res_r, lse_s, lse_r, mx_s, mx_r, at_s, at_r,
):
    s = lax.axis_index("slot")
    p = lax.axis_index("space")
    half = lax.rem(s, 2)
    rank = s // 2
    partner = s + 1 - 2 * half
    twin = p + 1 - 2 * lax.rem(p, 2)
    lane = lambda shape: lax.broadcasted_iota(jnp.int32, shape, 1)
    line = lambda shape: lax.broadcasted_iota(jnp.int32, shape, 0)

    def head_of(index):
        return old_hbm.at[:, pl.ds(pl.multiple_of(index * TOK, TOK), TOK)]

    q_copy = pltpu.make_async_copy(q_hbm.at[pl.ds(pl.multiple_of(half * TQ, TQ), TQ), :], qv, lsem)
    q_copy.start()
    raw_copy = pltpu.make_async_copy(raw_hbm, rawv, lsem2)
    raw_copy.start()
    kv_copy = pltpu.make_async_copy(head_of(p), kv.at[0, p], lsem3)
    kv_copy.start()
    w_copy = pltpu.make_async_copy(w_hbm, wv, lsem4)
    w_copy.start()

    barrier = pltpu.get_barrier_semaphore()

    def greet(slot, space):
        pl.semaphore_signal(barrier, inc=1, device_id=to(slot, space), device_id_type=MESH)

    for d in range(1, N):
        greet(s, lax.rem(p + d, N))
    for d in range(1, N):
        greet(partner, lax.rem(p + d, N))
    for d in range(1, N):
        greet(lax.rem(s + d, N), p)
    greet(twin, s)
    greet(p, partner)

    @pl.when(s != p)
    def _():
        greet(p, s)

    q_copy.wait()
    for c in range(PAIRS):
        qt[c * 128 : (c + 1) * 128, :] = qv[:, c * 128 : (c + 1) * 128].T

    row_i = line((256, N * HD))
    col_i = lane((256, N * HD))
    sel[...] = jnp.where(row_i % 128 == col_i // HD, 1.0, 0.0).astype(BF16)
    ones_row = jnp.where(line((HD, TQ)) == 0, 1.0, 0.0).astype(BF16)
    for b in range(N):
        qa[b, 3 * HD :, :] = ones_row

    @pl.when(s != p)
    def _():
        pl.semaphore_wait(barrier, 3 * (N - 1) + 3)

    @pl.when(s == p)
    def _():
        pl.semaphore_wait(barrier, 3 * (N - 1) + 2)

    @pl.when(p < N - 1)
    def _():
        remote(raw_hbm.at[:, 1], halo, halo_s, halo_r, s, p + 1).start()

    def move_on(i):
        @pl.when(s < N - 1)
        def _():
            part = pl.ds(i * (TOK // 8), TOK // 8)
            remote(old_hbm.at[part, :], aged.at[part, :], ag_s, ag_r, s + 1, p).start()

    for d in range(1, N):
        peer = lax.rem(p + d, N)
        remote(head_of(peer), kv.at[0, p], kv_s, kv_r, s, peer).start()
        if d % 4 == 0:
            move_on(d // 4 - 1)
    for d in range(1, N):
        peer = lax.rem(p + d, N)
        remote(
            qt.at[pl.ds(pl.multiple_of(peer * HD, HD), HD), :], qall.at[p], q_s, q_r.at[p], s, peer
        ).start()
        if d % 3 == 0:
            move_on(d // 3 + 2)

    for d in range(N):
        peer = lax.rem(p + d, N)
        remote(head_of(peer), kv.at[1, p], kx_s, kx_r, partner, peer).start()

    @pl.when(s == 0)
    def _():
        zeros[...] = jnp.zeros_like(zeros)
        pltpu.make_async_copy(zeros, aged, lsem5).start()

    raw_copy.wait()

    @pl.when(p > 0)
    def _():
        wait_bytes(halo, halo_r)

    @pl.when(p == 0)
    def _():
        halo[...] = jnp.zeros_like(halo)

    edge = jnp.zeros((8, 8, 128), F32)
    for b in range(3):
        xf[b, :, 0:8, :] = edge
        xf[b, :, 8:, :] = (halo[...] if b == 0 else rawv[:, b - 1]).astype(F32)
    weight = pw_ref[...].astype(F32)
    key = lane((MC, 128)) < HD
    for f in range(4):
        total = jnp.zeros((MC, 128), F32)
        for a in range(3):
            frame = 2 * f + a - 1
            if frame < 0:
                continue
            for b in range(3):
                for g in range(3):
                    tap = 9 * a + 3 * b + g
                    total += weight[tap : tap + 1, :] * xf[b, frame, pl.ds(7 + g, MC, stride=2), :]
        mean_lo = jnp.sum(jnp.where(key, total, 0.0), axis=1, keepdims=True) / HD
        mean_hi = jnp.sum(jnp.where(key, 0.0, total), axis=1, keepdims=True) / HD
        centred = total - jnp.where(key, mean_lo, mean_hi)
        square = centred * centred
        var_lo = jnp.sum(jnp.where(key, square, 0.0), axis=1, keepdims=True) / HD
        var_hi = jnp.sum(jnp.where(key, 0.0, square), axis=1, keepdims=True) / HD
        normed = centred * lax.rsqrt(jnp.where(key, var_lo, var_hi) + 1e-06)
        fresh[f * MC : (f + 1) * MC, :] = normed.astype(BF16)

    @pl.when(s != p)
    def _():
        remote(fresh, kv.at[0, N], fr_s, fr_r, p, s).start()

    @pl.when(s == p)
    def _():
        kv[0, N] = fresh[...]

    remote(fresh, kv.at[1, N], fx_s, fx_r, twin, s).start()

    qall[p] = qt[pl.ds(pl.multiple_of(p * HD, HD), HD), :]

    def prepare(k, i, count):
        x = kv[k, i].astype(F32)
        turned = pltpu.roll(x, HD, 1)
        low = lane((TOK, TOK)) < HD
        column = line((TOK, TOK)) % MC
        mask = jnp.where((lane((TOK, TOK)) == HD) & (column >= count), MASKED, 0.0)
        row = pl.ds(pl.multiple_of(i * TOK, TOK), TOK)
        kaug[k, row, 0:128] = jnp.where(low, x, turned).astype(BF16)
        kaug[k, row, 128:256] = jnp.where(low, x, mask).astype(BF16)
        upper = line((TOK, TOK)) < HD
        vt[k, :, row] = jnp.where(upper, 1.0, x.T).astype(BF16)

    def prepare_slot(k, count):
        def one(i, carry):
            prepare(k, i, count)
            return carry

        lax.fori_loop(0, N, one, 0)

    scale = HD ** (-0.5) * math.log2(math.e)
    pair0 = p // 2

    def pair_of(i):
        return lax.rem(pair0 - i + 2 * PAIRS, PAIRS)

    def block_of(i, t):
        return 2 * pair_of(2 * i + t // 2) + t % 2

    def build(b):
        x = qall[b].astype(F32) * scale
        first = x.astype(BF16)
        x = x - first.astype(F32)
        second = x.astype(BF16)
        x = x - second.astype(F32)
        qa[b, 0:HD, :] = first
        qa[b, HD : 2 * HD, :] = second
        qa[b, 2 * HD : 3 * HD, :] = x.astype(BF16)

    def scores(k, b, z):
        peak = None
        for c in range(0, NK, 128):
            block = jnp.dot(kaug[k, c : c + 128, :], qa[b], preferred_element_type=F32)
            S[z, c : c + 128, :] = block
            top = jnp.max(block.reshape(16, 8, TQ), axis=0)
            peak = top if peak is None else jnp.maximum(peak, top)
        return peak

    def weigh(k, z, peak):
        top = jnp.max(peak, axis=0, keepdims=True)
        total = None
        for c in range(0, NK, 256):
            n = min(256, NK - c)
            weights = jnp.exp2(S[z, c : c + n, :] - top).astype(BF16)
            part = jnp.dot(vt[k, :, c : c + n], weights, preferred_element_type=F32)
            total = part if total is None else total + part
        return top, total

    def queries_of(pair):
        wait_bytes(qall.at[0], q_r.at[2 * pair])
        wait_bytes(qall.at[0], q_r.at[2 * pair + 1])

    kv_copy.wait()
    wait_bytes(kv.at[0, pl.ds(0, N - 1)], kv_r)
    prepare_slot(0, valid[s + 1])

    @pl.when(s != p)
    def _():
        wait_bytes(kv.at[0, N], fr_r)

    prepare(0, N, valid[0])
    wait_bytes(qall.at[0], q_r.at[twin])
    queries_of(pair_of(1))
    for t in range(4):
        build(block_of(0, t))
    first_peak = scores(0, block_of(0, 0), 0)

    def own_step(i, peak):
        @pl.when(i < 3)
        def _():
            queries_of(pair_of(2 * i + 2))
            queries_of(pair_of(2 * i + 3))

        for t in range(4):
            b = block_of(i, t)
            build(block_of(i + 1, t))
            later = scores(0, block_of(i, t + 1) if t < 3 else block_of(i + 1, 0), (t + 1) % 2)
            top, total = weigh(0, t % 2, peak)
            st[b] = total
            sm[pl.ds(b, 1), :] = top
            peak = later
        return peak

    lax.fori_loop(0, 4, own_step, first_peak)

    wait_bytes(kv.at[1, pl.ds(0, N)], kx_r)
    prepare_slot(1, valid[partner + 1])
    wait_bytes(kv.at[1, N], fx_r)
    prepare(1, N, valid[0])
    first_peak = scores(1, block_of(0, 0), 0)

    def partner_step(i, peak):
        for t in range(4):
            b = block_of(i, t)
            later = scores(1, block_of(i, t + 1) if t < 3 else block_of(i + 1, 0), (t + 1) % 2)
            top, total = weigh(1, t % 2, peak)
            before = sm[pl.ds(b, 1), :]
            both = jnp.maximum(top, before)
            total = total * jnp.exp2(top - both) + st[b] * jnp.exp2(before - both)
            ot[t // 2, (t % 2) * HD : (t % 2 + 1) * HD, :] = total[HD:, :] / total[:HD, :]
            lt[pl.ds(b, 1), :] = both + jnp.log2(total[0:1, :])
            peak = later
        for u in range(2):
            sb[pair_of(2 * i + u)] = ot[u].T.astype(BF16).reshape(PAIRS, OWN, 128)
        for u in range(2):
            pair = pair_of(2 * i + u)
            for d in range(1, PAIRS):
                owner = lax.rem(rank + d, PAIRS)
                remote(sb.at[pair, owner], rb.at[rank, pair], res_s, res_r, 2 * owner + half, p).start()
        return peak

    lax.fori_loop(0, 4, partner_step, first_peak)

    lse = lt[...]
    first = lse.astype(BF16).astype(F32)
    second = (lse - first).astype(BF16).astype(F32)
    third = lse - first - second
    stacked = jnp.concatenate([first, second, third, jnp.zeros((128 - 3 * N, TQ), F32)], axis=0)
    ls[...] = stacked.T.astype(BF16).reshape(PAIRS, OWN, 128)
    for d in range(1, PAIRS):
        owner = lax.rem(rank + d, PAIRS)
        remote(ls.at[owner], lr.at[rank], lse_s, lse_r, 2 * owner + half, p).start()
    lr[rank] = ls[rank]
    rb[rank] = sb[:, rank]

    wait_bytes(lr.at[pl.ds(0, PAIRS - 1)], lse_r)
    parts = lr[...].astype(F32).reshape(PAIRS * OWN, 128)
    parts = parts + pltpu.roll(parts, 128 - N, 1) + pltpu.roll(parts, 128 - 2 * N, 1)
    parts = jnp.where(lane((PAIRS * OWN, 128)) < N, parts, 0.0).reshape(PAIRS, OWN, 128)
    share = jnp.exp2(parts - jnp.max(parts, axis=0, keepdims=True))
    share = (share / jnp.sum(share, axis=0, keepdims=True)).reshape(PAIRS * OWN, 128)
    share_hi = share.astype(BF16)
    share_lo = (share - share_hi.astype(F32)).astype(BF16)
    shares = jnp.concatenate([share_hi, share_lo], axis=1)
    wait_bytes(rb.at[pl.ds(0, PAIRS - 1)], res_r)
    for j in range(PAIRS):
        spread = jnp.dot(shares, sel[:, j * 128 : (j + 1) * 128], preferred_element_type=F32)
        mixed = jnp.sum(spread.reshape(PAIRS, OWN, 128) * rb[:, j].astype(F32), axis=0)
        mx[j] = mixed.astype(BF16)

    for d in range(1, N):
        peer = lax.rem(p + d, N)
        remote(mx.at[peer // 2], mr.at[p], mx_s, mx_r, s, peer).start()
    mr[p] = mx[p // 2]
    w_copy.wait()
    wait_bytes(mr.at[pl.ds(0, N - 1)], mx_r)
    odd = lax.rem(p, 2) == 1
    left = lane((OWN, 128)) < HD
    pieces = []
    for j in range(PAIRS):
        a = mr[2 * j].astype(F32)
        b = mr[2 * j + 1].astype(F32)
        a = jnp.where(odd, pltpu.roll(a, HD, 1), a)
        b = jnp.where(odd, b, pltpu.roll(b, HD, 1))
        pieces.append(jnp.where(left, a, b).astype(BF16))
    heads = jnp.concatenate(pieces, axis=1)
    att[...] = jnp.dot(heads, wv[...], preferred_element_type=F32).astype(BF16)

    y, z = s // RING, lax.rem(s, RING)
    PART = OWN // CUT

    def start_of(index, c):
        return pl.multiple_of((lax.rem(index, 2) * PAIRS + index // 2) * OWN + c * PART, PART)

    def rows(index, c):
        return out.at[pl.ds(start_of(index, c), PART), :]

    def near(dz):
        return y * RING + lax.rem(z + dz + RING, RING)

    def far(dz):
        return (1 - y) * RING + lax.rem(z + dz + RING, RING)

    sent = [0]

    def push(index, target, c, src=None):
        remote(
            rows(index, c) if src is None else src, rows(index, c), at_s.at[sent[0]], at_r.at[CUT * index + c], target, p
        ).start()
        sent[0] += 1

    def got(index, c):
        wait_bytes(rows(0, 0), at_r.at[CUT * index + c])

    for c in range(CUT):
        push(s, far(0), c, att.at[c * PART : (c + 1) * PART, :])
    for c in range(CUT):
        push(s, near(1), c, att.at[c * PART : (c + 1) * PART, :])
        push(s, near(-1), c, att.at[c * PART : (c + 1) * PART, :])
        out[pl.ds(start_of(s, c), PART), :] = att[c * PART : (c + 1) * PART, :]

    def pass_far(c):
        got(far(0), c)
        push(far(0), near(1), c)
        push(far(0), near(-1), c)

    def pass_near(k, c):
        got(near(-k), c)
        if k < 4:
            push(near(-k), near(1), c)
            got(near(k), c)
        if k < 3:
            push(near(k), near(-1), c)

    def pass_far_on(k, c):
        got(far(k), c)
        if k < 4:
            push(far(k), near(-1), c)
            got(far(-k), c)
        if k < 3:
            push(far(-k), near(1), c)

    for c in range(CUT):
        pass_near(1, c)
    for c in range(CUT):
        pass_far(c)
    for k in range(2, 5):
        for c in range(CUT):
            pass_near(k, c)
        for c in range(CUT):
            pass_far_on(k - 1, c)
    for c in range(CUT):
        pass_far_on(4, c)

    for i in range(sent[0]):
        wait_bytes(rows(0, 0), at_s.at[i])
    wait_bytes(kv.at[0, pl.ds(0, N - 1)], kv_s)
    wait_bytes(kv.at[1, pl.ds(0, N)], kx_s)
    wait_bytes(qall.at[pl.ds(0, N - 1)], q_s)
    wait_bytes(rb.at[pl.ds(0, PAIRS - 1)], res_s)
    wait_bytes(lr.at[pl.ds(0, PAIRS - 1)], lse_s)
    wait_bytes(mr.at[pl.ds(0, N - 1)], mx_s)
    wait_bytes(kv.at[1, N], fx_s)

    @pl.when(p < N - 1)
    def _():
        wait_bytes(halo, halo_s)

    @pl.when(s != p)
    def _():
        wait_bytes(kv.at[0, N], fr_s)

    @pl.when(s < N - 1)
    def _():
        wait_bytes(old_hbm, ag_s)

    @pl.when(s > 0)
    def _():
        wait_bytes(old_hbm, ag_r)

    @pl.when(s == 0)
    def _():
        pltpu.make_async_copy(zeros, aged, lsem5).wait()


def local(queries, raw_clip, pool_weight, old_memory, valid_columns, out_weight):
    dma = pltpu.SemaphoreType.DMA
    anywhere = pl.BlockSpec(memory_space=pl.ANY)
    vmem = pl.BlockSpec(memory_space=pltpu.VMEM)
    attended, fresh, aged = pl.pallas_call(
        kernel,
        out_shape=(
            jax.ShapeDtypeStruct((QB, N * HD), BF16),
            jax.ShapeDtypeStruct((TOK, TOK), BF16),
            jax.ShapeDtypeStruct((TOK, N * TOK), BF16),
        ),
        in_specs=[anywhere, anywhere, vmem, anywhere, pl.BlockSpec(memory_space=pltpu.SMEM), anywhere],
        out_specs=(vmem, vmem, anywhere),
        scratch_shapes=[
            pltpu.VMEM((TQ, N * HD), BF16),
            pltpu.VMEM((N * HD, TQ), BF16),
            pltpu.VMEM((N, HD, TQ), BF16),
            pltpu.VMEM((2, N + 1, TOK, TOK), BF16),
            pltpu.VMEM((2, NK, 256), BF16),
            pltpu.VMEM((2, 128, NK), BF16),
            pltpu.VMEM((2, NK, TQ), F32),
            pltpu.VMEM((N, 256, TQ), BF16),
            pltpu.VMEM((N, 128, TQ), F32),
            pltpu.VMEM((N, TQ), F32),
            pltpu.VMEM((2, 128, TQ), F32),
            pltpu.VMEM((N, TQ), F32),
            pltpu.VMEM((PAIRS, PAIRS, OWN, 128), BF16),
            pltpu.VMEM((PAIRS, PAIRS, OWN, 128), BF16),
            pltpu.VMEM((PAIRS, OWN, 128), BF16),
            pltpu.VMEM((PAIRS, OWN, 128), BF16),
            pltpu.VMEM((PAIRS, OWN, 128), BF16),
            pltpu.VMEM((N, OWN, 128), BF16),
            pltpu.VMEM((OWN, N * HD), BF16),
            pltpu.VMEM((256, N * HD), BF16),
            pltpu.VMEM((N * HD, N * HD), BF16),
            pltpu.VMEM((8, 2, 64, 128), BF16),
            pltpu.VMEM((8, 64, 128), BF16),
            pltpu.VMEM((3, 8, 72, 128), F32),
            pltpu.VMEM((TOK, N * TOK), BF16),
            *[dma] * 5,
            *[dma] * 7,
            dma((N,)),
            *[dma] * 12,
            dma((N * CUT,)),
            dma((N * CUT,)),
        ],
        compiler_params=pltpu.CompilerParams(
            collective_id=0, has_side_effects=True, vmem_limit_bytes=60 * 1024 * 1024
        ),
        name="attend",
    )(
        queries,
        raw_clip,
        pool_weight,
        old_memory.reshape(TOK, N * TOK),
        valid_columns,
        out_weight,
    )
    return (attended, fresh.reshape(4, 1, MC, TOK), aged.reshape(old_memory.shape))


def solution(mesh):
    return jax.shard_map(
        local,
        mesh=mesh,
        in_specs=(
            P("space", None),
            P(None, "space", None, "slot"),
            P(None, "slot"),
            P("slot", None, "space", None, None),
            P(),
            P(),
        ),
        out_specs=(
            P("space", None),
            P(None, "space", None, "slot"),
            P("slot", None, "space", None, None),
        ),
        check_vma=False,
    )
```

```python
import math

import jax
import jax.numpy as jnp
from jax import lax
from jax.experimental import pallas as pl
from jax.experimental.pallas import tpu as pltpu
from jax.sharding import PartitionSpec as P

F32 = jnp.float32
BF16 = jnp.bfloat16
MESH = pl.DeviceIdType.MESH
N = 16
HD = 64
TOK = 128
QB = 512
NK = (N * TOK, (N + 2) * TOK)
TQ = 256
MC = 32
MASKED = -1e30
PAIRS = N // 2
OWN = QB // N
RING = 8
CUT = 2


def to(slot, space):
    return {"slot": slot, "space": space}


def remote(src, dst, send, recv, slot, space):
    return pltpu.make_async_remote_copy(
        src_ref=src, dst_ref=dst, send_sem=send, recv_sem=recv, device_id=to(slot, space), device_id_type=MESH
    )


def wait_bytes(ref, sem):
    pltpu.make_async_copy(ref, ref, sem).wait()


def kernel(
    q_hbm, raw_hbm, pw_ref, old_hbm, valid, w_hbm,
    out, fresh, aged,
    qv, qt, qall, kv0, kv1, kaug0, kaug1, vt0, vt1, S, qa, st, sm, ot, lt, sb, rb, ls, lr, mx, mr, att, sel, wv, rawv, halo, xf, zeros,
    lsem, lsem2, lsem3, lsem4, lsem5,
    halo_s, halo_r, kv_s, kv_r, kx_s, kx_r, q_s, q_r, fr_s, fr_r, fx_s, fx_r, ag_s, ag_r,
    res_s, res_r, lse_s, lse_r, mx_s, mx_r, at_s, at_r,
):
    s = lax.axis_index("slot")
    p = lax.axis_index("space")
    half = lax.rem(s, 2)
    rank = s // 2
    partner = s + 1 - 2 * half
    twin = p + 1 - 2 * lax.rem(p, 2)
    kv, kaug, vt = (kv0, kv1), (kaug0, kaug1), (vt0, vt1)
    lane = lambda shape: lax.broadcasted_iota(jnp.int32, shape, 1)
    line = lambda shape: lax.broadcasted_iota(jnp.int32, shape, 0)

    def head_of(index):
        return old_hbm.at[:, pl.ds(pl.multiple_of(index * TOK, TOK), TOK)]

    q_copy = pltpu.make_async_copy(q_hbm.at[pl.ds(pl.multiple_of(half * TQ, TQ), TQ), :], qv, lsem)
    q_copy.start()
    raw_copy = pltpu.make_async_copy(raw_hbm, rawv, lsem2)
    raw_copy.start()
    kv_copy = pltpu.make_async_copy(head_of(p), kv0.at[p], lsem3)
    kv_copy.start()
    w_copy = pltpu.make_async_copy(w_hbm, wv, lsem4)
    w_copy.start()

    barrier = pltpu.get_barrier_semaphore()

    def greet(slot, space):
        pl.semaphore_signal(barrier, inc=1, device_id=to(slot, space), device_id_type=MESH)

    for d in range(1, N):
        greet(s, lax.rem(p + d, N))
    for d in range(1, N):
        greet(lax.rem(s + d, N), p)
    greet(twin, s)
    greet(p, partner)

    @pl.when(s != p)
    def _():
        greet(p, s)

    q_copy.wait()
    for c in range(PAIRS):
        qt[c * 128 : (c + 1) * 128, :] = qv[:, c * 128 : (c + 1) * 128].T

    row_i = line((256, N * HD))
    col_i = lane((256, N * HD))
    sel[...] = jnp.where(row_i % 128 == col_i // HD, 1.0, 0.0).astype(BF16)
    ones_row = jnp.where(line((HD, TQ)) == 0, 1.0, 0.0).astype(BF16)
    for b in range(N):
        qa[b, 3 * HD :, :] = ones_row

    @pl.when(s != p)
    def _():
        pl.semaphore_wait(barrier, 2 * (N - 1) + 3)

    @pl.when(s == p)
    def _():
        pl.semaphore_wait(barrier, 2 * (N - 1) + 2)

    @pl.when(p < N - 1)
    def _():
        remote(raw_hbm.at[:, 1], halo, halo_s, halo_r, s, p + 1).start()

    for d in range(1, N):
        peer = lax.rem(p + d, N)
        remote(head_of(peer), kv0.at[p], kv_s, kv_r, s, peer).start()

    def ask(peer):
        remote(qt.at[pl.ds(pl.multiple_of(peer * HD, HD), HD), :], qall.at[p], q_s, q_r.at[p], s, peer).start()

    def ask_pair(k):
        for b in range(2):
            ask(2 * lax.rem(p // 2 + k, PAIRS) + b)

    ask(twin)
    ask_pair(1)

    def move_on():
        remote(old_hbm, aged, ag_s, ag_r, s + 1, p).start()

    @pl.when((s != RING - 1) & (s < N - 1))
    def _():
        move_on()

    @pl.when(s == 0)
    def _():
        zeros[...] = jnp.zeros_like(zeros)
        pltpu.make_async_copy(zeros, aged, lsem5).start()

    raw_copy.wait()

    @pl.when(p > 0)
    def _():
        wait_bytes(halo, halo_r)

    @pl.when(p == 0)
    def _():
        halo[...] = jnp.zeros_like(halo)

    edge = jnp.zeros((8, 8, 128), F32)
    for b in range(3):
        xf[b, :, 0:8, :] = edge
        xf[b, :, 8:, :] = (halo[...] if b == 0 else rawv[:, b - 1]).astype(F32)
    weight = pw_ref[...].astype(F32)
    key = lane((MC, 128)) < HD
    for f in range(4):
        total = jnp.zeros((MC, 128), F32)
        for a in range(3):
            frame = 2 * f + a - 1
            if frame < 0:
                continue
            for b in range(3):
                for g in range(3):
                    tap = 9 * a + 3 * b + g
                    total += weight[tap : tap + 1, :] * xf[b, frame, pl.ds(7 + g, MC, stride=2), :]
        mean_lo = jnp.sum(jnp.where(key, total, 0.0), axis=1, keepdims=True) / HD
        mean_hi = jnp.sum(jnp.where(key, 0.0, total), axis=1, keepdims=True) / HD
        centred = total - jnp.where(key, mean_lo, mean_hi)
        square = centred * centred
        var_lo = jnp.sum(jnp.where(key, square, 0.0), axis=1, keepdims=True) / HD
        var_hi = jnp.sum(jnp.where(key, 0.0, square), axis=1, keepdims=True) / HD
        normed = centred * lax.rsqrt(jnp.where(key, var_lo, var_hi) + 1e-06)
        fresh[f * MC : (f + 1) * MC, :] = normed.astype(BF16)

    qall[p] = qt[pl.ds(pl.multiple_of(p * HD, HD), HD), :]

    def prepare(k, i, count):
        x = kv[k][i].astype(F32)
        turned = pltpu.roll(x, HD, 1)
        low = lane((TOK, TOK)) < HD
        column = line((TOK, TOK)) % MC
        mask = jnp.where((lane((TOK, TOK)) == HD) & (column >= count), MASKED, 0.0)
        row = pl.ds(pl.multiple_of(i * TOK, TOK), TOK)
        kaug[k][row, 0:128] = jnp.where(low, x, turned).astype(BF16)
        kaug[k][row, 128:256] = jnp.where(low, x, mask).astype(BF16)
        upper = line((TOK, TOK)) < HD
        vt[k][:, row] = jnp.where(upper, 1.0, x.T).astype(BF16)

    def prepare_slot(k, count):
        def one(i, carry):
            prepare(k, i, count)
            return carry

        lax.fori_loop(0, N, one, 0)

    scale = HD ** (-0.5) * math.log2(math.e)
    pair0 = p // 2

    def pair_of(i):
        return lax.rem(pair0 - i + 2 * PAIRS, PAIRS)

    def block_of(i, t):
        return 2 * pair_of(2 * i + t // 2) + t % 2

    def build(b):
        x = qall[b].astype(F32) * scale
        first = x.astype(BF16)
        x = x - first.astype(F32)
        second = x.astype(BF16)
        x = x - second.astype(F32)
        qa[b, 0:HD, :] = first
        qa[b, HD : 2 * HD, :] = second
        qa[b, 2 * HD : 3 * HD, :] = x.astype(BF16)

    def scores(k, b, z):
        peak = None
        for c in range(0, NK[k], 128):
            block = jnp.dot(kaug[k][c : c + 128, :], qa[b], preferred_element_type=F32)
            S[z, c : c + 128, :] = block
            top = jnp.max(block.reshape(16, 8, TQ), axis=0)
            peak = top if peak is None else jnp.maximum(peak, top)
        return peak

    def weigh(k, z, peak):
        top = jnp.max(peak, axis=0, keepdims=True)
        total = None
        for c in range(0, NK[k], 256):
            weights = jnp.exp2(S[z, c : c + 256, :] - top).astype(BF16)
            part = jnp.dot(vt[k][:, c : c + 256], weights, preferred_element_type=F32)
            total = part if total is None else total + part
        return top, total

    def queries_of(pair):
        wait_bytes(qall.at[0], q_r.at[2 * pair])
        wait_bytes(qall.at[0], q_r.at[2 * pair + 1])

    kv_copy.wait()
    wait_bytes(kv0.at[pl.ds(0, N - 1)], kv_r)

    remote(kv0, kv1.at[pl.ds(0, N)], kx_s, kx_r, partner, p).start()
    for k in range(2, PAIRS):
        ask_pair(k)

    @pl.when(s != p)
    def _():
        remote(fresh, kv1.at[N], fr_s, fr_r, p, s).start()

    @pl.when(s == p)
    def _():
        kv1[N] = fresh[...]

    remote(fresh, kv1.at[N + 1], fx_s, fx_r, twin, s).start()

    prepare_slot(0, valid[s + 1])
    wait_bytes(qall.at[0], q_r.at[twin])
    queries_of(pair_of(1))
    for t in range(4):
        build(block_of(0, t))
    first_peak = scores(0, block_of(0, 0), 0)

    def own_step(i, peak):
        @pl.when((i == 3) & (s == RING - 1))
        def _():
            move_on()

        @pl.when(i < 3)
        def _():
            queries_of(pair_of(2 * i + 2))
            queries_of(pair_of(2 * i + 3))

        for t in range(4):
            b = block_of(i, t)
            build(block_of(i + 1, t))
            later = scores(0, block_of(i, t + 1) if t < 3 else block_of(i + 1, 0), (t + 1) % 2)
            top, total = weigh(0, t % 2, peak)
            st[b] = total
            sm[pl.ds(b, 1), :] = top
            peak = later
        return peak

    lax.fori_loop(0, 4, own_step, first_peak)

    wait_bytes(kv1.at[pl.ds(0, N)], kx_r)
    prepare_slot(1, valid[partner + 1])

    @pl.when(s != p)
    def _():
        wait_bytes(kv1.at[N], fr_r)

    prepare(1, N, valid[0])
    wait_bytes(kv1.at[N + 1], fx_r)
    prepare(1, N + 1, valid[0])
    first_peak = scores(1, block_of(0, 0), 0)

    def partner_step(i, peak):
        for t in range(4):
            b = block_of(i, t)
            later = scores(1, block_of(i, t + 1) if t < 3 else block_of(i + 1, 0), (t + 1) % 2)
            top, total = weigh(1, t % 2, peak)
            before = sm[pl.ds(b, 1), :]
            both = jnp.maximum(top, before)
            total = total * jnp.exp2(top - both) + st[b] * jnp.exp2(before - both)
            ot[t // 2, (t % 2) * HD : (t % 2 + 1) * HD, :] = total[HD:, :] / total[:HD, :]
            lt[pl.ds(b, 1), :] = both + jnp.log2(total[0:1, :])
            peak = later
        for u in range(2):
            sb[pair_of(2 * i + u)] = ot[u].T.astype(BF16).reshape(PAIRS, OWN, 128)
        for u in range(2):
            pair = pair_of(2 * i + u)
            for d in range(1, PAIRS):
                owner = lax.rem(rank + d, PAIRS)
                remote(sb.at[pair, owner], rb.at[rank, pair], res_s, res_r, 2 * owner + half, p).start()
        return peak

    lax.fori_loop(0, 4, partner_step, first_peak)

    lse = lt[...]
    first = lse.astype(BF16).astype(F32)
    second = (lse - first).astype(BF16).astype(F32)
    third = lse - first - second
    stacked = jnp.concatenate([first, second, third, jnp.zeros((128 - 3 * N, TQ), F32)], axis=0)
    ls[...] = stacked.T.astype(BF16).reshape(PAIRS, OWN, 128)
    for d in range(1, PAIRS):
        owner = lax.rem(rank + d, PAIRS)
        remote(ls.at[owner], lr.at[rank], lse_s, lse_r, 2 * owner + half, p).start()
    lr[rank] = ls[rank]
    rb[rank] = sb[:, rank]

    wait_bytes(lr.at[pl.ds(0, PAIRS - 1)], lse_r)
    parts = lr[...].astype(F32).reshape(PAIRS * OWN, 128)
    parts = parts + pltpu.roll(parts, 128 - N, 1) + pltpu.roll(parts, 128 - 2 * N, 1)
    parts = jnp.where(lane((PAIRS * OWN, 128)) < N, parts, 0.0).reshape(PAIRS, OWN, 128)
    share = jnp.exp2(parts - jnp.max(parts, axis=0, keepdims=True))
    share = (share / jnp.sum(share, axis=0, keepdims=True)).reshape(PAIRS * OWN, 128)
    share_hi = share.astype(BF16)
    share_lo = (share - share_hi.astype(F32)).astype(BF16)
    shares = jnp.concatenate([share_hi, share_lo], axis=1)
    wait_bytes(rb.at[pl.ds(0, PAIRS - 1)], res_r)
    for j in range(PAIRS):
        spread = jnp.dot(shares, sel[:, j * 128 : (j + 1) * 128], preferred_element_type=F32)
        mixed = jnp.sum(spread.reshape(PAIRS, OWN, 128) * rb[:, j].astype(F32), axis=0)
        mx[j] = mixed.astype(BF16)

    for d in range(1, N):
        peer = lax.rem(p + d, N)
        remote(mx.at[peer // 2], mr.at[p], mx_s, mx_r, s, peer).start()
    mr[p] = mx[p // 2]
    w_copy.wait()
    wait_bytes(mr.at[pl.ds(0, N - 1)], mx_r)
    odd = lax.rem(p, 2) == 1
    left = lane((OWN, 128)) < HD
    pieces = []
    for j in range(PAIRS):
        a = mr[2 * j].astype(F32)
        b = mr[2 * j + 1].astype(F32)
        a = jnp.where(odd, pltpu.roll(a, HD, 1), a)
        b = jnp.where(odd, b, pltpu.roll(b, HD, 1))
        pieces.append(jnp.where(left, a, b).astype(BF16))
    heads = jnp.concatenate(pieces, axis=1)
    att[...] = jnp.dot(heads, wv[...], preferred_element_type=F32).astype(BF16)

    y, z = s // RING, lax.rem(s, RING)
    PART = OWN // CUT

    def start_of(index, c):
        return pl.multiple_of((lax.rem(index, 2) * PAIRS + index // 2) * OWN + c * PART, PART)

    def rows(index, c):
        return out.at[pl.ds(start_of(index, c), PART), :]

    def near(dz):
        return y * RING + lax.rem(z + dz + RING, RING)

    def far(dz):
        return (1 - y) * RING + lax.rem(z + dz + RING, RING)

    sent = [0]

    def push(index, target, c, src=None):
        remote(
            rows(index, c) if src is None else src, rows(index, c), at_s.at[sent[0]], at_r.at[CUT * index + c], target, p
        ).start()
        sent[0] += 1

    def got(index, c):
        wait_bytes(rows(0, 0), at_r.at[CUT * index + c])

    for c in range(CUT):
        push(s, far(0), c, att.at[c * PART : (c + 1) * PART, :])
    for c in range(CUT):
        push(s, near(1), c, att.at[c * PART : (c + 1) * PART, :])
        push(s, near(-1), c, att.at[c * PART : (c + 1) * PART, :])
        out[pl.ds(start_of(s, c), PART), :] = att[c * PART : (c + 1) * PART, :]

    def pass_far(c):
        got(far(0), c)
        push(far(0), near(1), c)
        push(far(0), near(-1), c)

    def pass_near(k, c):
        got(near(-k), c)
        if k < 4:
            push(near(-k), near(1), c)
            got(near(k), c)
        if k < 3:
            push(near(k), near(-1), c)

    def pass_far_on(k, c):
        got(far(k), c)
        if k < 4:
            push(far(k), near(-1), c)
            got(far(-k), c)
        if k < 3:
            push(far(-k), near(1), c)

    for c in range(CUT):
        pass_near(1, c)
    for c in range(CUT):
        pass_far(c)
    for k in range(2, 5):
        for c in range(CUT):
            pass_near(k, c)
        for c in range(CUT):
            pass_far_on(k - 1, c)
    for c in range(CUT):
        pass_far_on(4, c)

    for i in range(sent[0]):
        wait_bytes(rows(0, 0), at_s.at[i])
    wait_bytes(kv0.at[pl.ds(0, N - 1)], kv_s)
    wait_bytes(kv1.at[pl.ds(0, N)], kx_s)
    wait_bytes(qall.at[pl.ds(0, N - 1)], q_s)
    wait_bytes(rb.at[pl.ds(0, PAIRS - 1)], res_s)
    wait_bytes(lr.at[pl.ds(0, PAIRS - 1)], lse_s)
    wait_bytes(mr.at[pl.ds(0, N - 1)], mx_s)
    wait_bytes(kv1.at[N + 1], fx_s)

    @pl.when(p < N - 1)
    def _():
        wait_bytes(halo, halo_s)

    @pl.when(s != p)
    def _():
        wait_bytes(kv1.at[N], fr_s)

    @pl.when(s < N - 1)
    def _():
        wait_bytes(old_hbm, ag_s)

    @pl.when(s > 0)
    def _():
        wait_bytes(old_hbm, ag_r)

    @pl.when(s == 0)
    def _():
        pltpu.make_async_copy(zeros, aged, lsem5).wait()


def settle(a, b, c, a_out, b_out, c_out, a_mid, b_mid, c_mid, ins, outs):
    moves = []
    for src, mid, dst, parts in zip((a, c, b), (a_mid, c_mid, b_mid), (a_out, c_out, b_out), (4, 2, 1)):
        rows = src.shape[0] // parts
        for i in range(parts):
            part = pl.ds(i * rows, rows)
            n = len(moves)
            moves.append(
                (
                    pltpu.make_async_copy(src.at[part, :], mid.at[part, :], ins.at[n]),
                    pltpu.make_async_copy(mid.at[part, :], dst.at[part, :], outs.at[n]),
                )
            )
    for first, _ in moves:
        first.start()
    for first, second in moves:
        first.wait()
        second.start()
    for _, second in moves:
        second.wait()


def local(queries, raw_clip, pool_weight, old_memory, valid_columns, out_weight):
    dma = pltpu.SemaphoreType.DMA
    anywhere = pl.BlockSpec(memory_space=pl.ANY)
    vmem = pl.BlockSpec(memory_space=pltpu.VMEM)
    attended, fresh, aged = pl.pallas_call(
        kernel,
        out_shape=(
            jax.ShapeDtypeStruct((QB, N * HD), BF16),
            jax.ShapeDtypeStruct((TOK, TOK), BF16),
            jax.ShapeDtypeStruct((TOK, N * TOK), BF16),
        ),
        in_specs=[anywhere, anywhere, vmem, anywhere, pl.BlockSpec(memory_space=pltpu.SMEM), anywhere],
        out_specs=(vmem, vmem, anywhere),
        scratch_shapes=[
            pltpu.VMEM((TQ, N * HD), BF16),
            pltpu.VMEM((N * HD, TQ), BF16),
            pltpu.VMEM((N, HD, TQ), BF16),
            pltpu.VMEM((N, TOK, TOK), BF16),
            pltpu.VMEM((N + 2, TOK, TOK), BF16),
            pltpu.VMEM((NK[0], 256), BF16),
            pltpu.VMEM((NK[1], 256), BF16),
            pltpu.VMEM((128, NK[0]), BF16),
            pltpu.VMEM((128, NK[1]), BF16),
            pltpu.VMEM((2, NK[1], TQ), F32),
            pltpu.VMEM((N, 256, TQ), BF16),
            pltpu.VMEM((N, 128, TQ), F32),
            pltpu.VMEM((N, TQ), F32),
            pltpu.VMEM((2, 128, TQ), F32),
            pltpu.VMEM((N, TQ), F32),
            pltpu.VMEM((PAIRS, PAIRS, OWN, 128), BF16),
            pltpu.VMEM((PAIRS, PAIRS, OWN, 128), BF16),
            pltpu.VMEM((PAIRS, OWN, 128), BF16),
            pltpu.VMEM((PAIRS, OWN, 128), BF16),
            pltpu.VMEM((PAIRS, OWN, 128), BF16),
            pltpu.VMEM((N, OWN, 128), BF16),
            pltpu.VMEM((OWN, N * HD), BF16),
            pltpu.VMEM((256, N * HD), BF16),
            pltpu.VMEM((N * HD, N * HD), BF16),
            pltpu.VMEM((8, 2, 64, 128), BF16),
            pltpu.VMEM((8, 64, 128), BF16),
            pltpu.VMEM((3, 8, 72, 128), F32),
            pltpu.VMEM((TOK, N * TOK), BF16),
            *[dma] * 5,
            *[dma] * 7,
            dma((N,)),
            *[dma] * 12,
            dma((N * CUT,)),
            dma((N * CUT,)),
        ],
        compiler_params=pltpu.CompilerParams(
            collective_id=0, has_side_effects=True, vmem_limit_bytes=60 * 1024 * 1024
        ),
        name="attend",
    )(
        queries,
        raw_clip,
        pool_weight,
        old_memory.reshape(TOK, N * TOK),
        valid_columns,
        out_weight,
    )
    shapes = tuple(jax.ShapeDtypeStruct(x.shape, x.dtype) for x in (attended, fresh, aged))
    attended, fresh, aged = pl.pallas_call(
        settle,
        out_shape=shapes,
        in_specs=[anywhere] * 3,
        out_specs=(anywhere,) * 3,
        scratch_shapes=[*(pltpu.VMEM(x.shape, x.dtype) for x in shapes), dma((7,)), dma((7,))],
        compiler_params=pltpu.CompilerParams(vmem_limit_bytes=60 * 1024 * 1024),
        name="settle",
    )(attended, fresh, aged)
    return (attended, fresh.reshape(4, 1, MC, TOK), aged.reshape(old_memory.shape))


def solution(mesh):
    return jax.shard_map(
        local,
        mesh=mesh,
        in_specs=(
            P("space", None),
            P(None, "space", None, "slot"),
            P(None, "slot"),
            P("slot", None, "space", None, None),
            P(),
            P(),
        ),
        out_specs=(
            P("space", None),
            P(None, "space", None, "slot"),
            P("slot", None, "space", None, None),
        ),
        check_vma=False,
    )
```

```python
import math

import jax
import jax.numpy as jnp
from jax import lax
from jax.experimental import pallas as pl
from jax.experimental.pallas import tpu as pltpu
from jax.sharding import PartitionSpec as P

F32 = jnp.float32
BF16 = jnp.bfloat16
MESH = pl.DeviceIdType.MESH
N = 16
HD = 64
TOK = 128
QB = 512
NK = (N * TOK, (N + 2) * TOK)
TQ = 256
MC = 32
MASKED = -1e30
PAIRS = N // 2
OWN = QB // N
PART = OWN // 2
RING = 8
CUT = 2


def to(slot, space):
    return {"slot": slot, "space": space}


def remote(src, dst, send, recv, slot, space):
    return pltpu.make_async_remote_copy(
        src_ref=src, dst_ref=dst, send_sem=send, recv_sem=recv, device_id=to(slot, space), device_id_type=MESH
    )


def wait_bytes(ref, sem):
    pltpu.make_async_copy(ref, ref, sem).wait()


def kernel(
    q_hbm, raw_hbm, pw_ref, old_hbm, valid, w_hbm,
    out, fresh, aged,
    qv, qt, qall, kv0, kv1, kaug0, kaug1, vt0, vt1, S, qa, st, sm, ot, lt, sb, rb, ls, lr, mx, mr, att, sel, wv, rawv, halo, xf, zeros,
    lsem, lsem2, lsem3, lsem4, lsem5,
    halo_s, halo_r, kv_s, kv_r, kx_s, kx_r, q_s, q_r, fr_s, fr_r, fx_s, fx_r, ag_s, ag_r,
    res_s, res_r, lse_s, lse_r, mx_s, mx_r, my_s, my_r, at_s, at_r,
):
    s = lax.axis_index("slot")
    p = lax.axis_index("space")
    half = lax.rem(s, 2)
    rank = s // 2
    partner = s + 1 - 2 * half
    twin = p + 1 - 2 * lax.rem(p, 2)
    y, z = s // RING, lax.rem(s, RING)
    across = lax.rem(s + RING, N)
    kv, kaug, vt = (kv0, kv1), (kaug0, kaug1), (vt0, vt1)
    lane = lambda shape: lax.broadcasted_iota(jnp.int32, shape, 1)
    line = lambda shape: lax.broadcasted_iota(jnp.int32, shape, 0)

    def head_of(index):
        return old_hbm.at[:, pl.ds(pl.multiple_of(index * TOK, TOK), TOK)]

    q_copy = pltpu.make_async_copy(q_hbm.at[pl.ds(pl.multiple_of(half * TQ, TQ), TQ), :], qv, lsem)
    q_copy.start()
    raw_copy = pltpu.make_async_copy(raw_hbm, rawv, lsem2)
    raw_copy.start()
    kv_copy = pltpu.make_async_copy(head_of(p), kv0.at[p], lsem3)
    kv_copy.start()
    w_copy = pltpu.make_async_copy(w_hbm, wv, lsem4)
    w_copy.start()

    barrier = pltpu.get_barrier_semaphore()

    def greet(slot, space):
        pl.semaphore_signal(barrier, inc=1, device_id=to(slot, space), device_id_type=MESH)

    for d in range(1, N):
        greet(s, lax.rem(p + d, N))
    for d in range(1, N):
        greet(across, lax.rem(p + d, N))
    for d in range(1, N):
        greet(lax.rem(s + d, N), p)
    greet(twin, s)
    greet(p, partner)

    @pl.when(s != p)
    def _():
        greet(p, s)

    q_copy.wait()
    for c in range(PAIRS):
        qt[c * 128 : (c + 1) * 128, :] = qv[:, c * 128 : (c + 1) * 128].T

    row_i = line((256, N * HD))
    col_i = lane((256, N * HD))
    sel[...] = jnp.where(row_i % 128 == col_i // HD, 1.0, 0.0).astype(BF16)
    ones_row = jnp.where(line((HD, TQ)) == 0, 1.0, 0.0).astype(BF16)
    for b in range(N):
        qa[b, 3 * HD :, :] = ones_row

    @pl.when(s != p)
    def _():
        pl.semaphore_wait(barrier, 3 * (N - 1) + 3)

    @pl.when(s == p)
    def _():
        pl.semaphore_wait(barrier, 3 * (N - 1) + 2)

    @pl.when(p < N - 1)
    def _():
        remote(raw_hbm.at[:, 1], halo, halo_s, halo_r, s, p + 1).start()

    for d in range(1, N):
        peer = lax.rem(p + d, N)
        remote(head_of(peer), kv0.at[p], kv_s, kv_r, s, peer).start()

    def ask(peer):
        remote(qt.at[pl.ds(pl.multiple_of(peer * HD, HD), HD), :], qall.at[p], q_s, q_r.at[p], s, peer).start()

    def ask_pair(k):
        for b in range(2):
            ask(2 * lax.rem(p // 2 + k, PAIRS) + b)

    ask(twin)
    ask_pair(1)

    def move_on():
        remote(old_hbm, aged, ag_s, ag_r, s + 1, p).start()

    @pl.when((s != RING - 1) & (s < N - 1))
    def _():
        move_on()

    @pl.when(s == 0)
    def _():
        zeros[...] = jnp.zeros_like(zeros)
        pltpu.make_async_copy(zeros, aged, lsem5).start()

    raw_copy.wait()

    @pl.when(p > 0)
    def _():
        wait_bytes(halo, halo_r)

    @pl.when(p == 0)
    def _():
        halo[...] = jnp.zeros_like(halo)

    edge = jnp.zeros((8, 8, 128), F32)
    for b in range(3):
        xf[b, :, 0:8, :] = edge
        xf[b, :, 8:, :] = (halo[...] if b == 0 else rawv[:, b - 1]).astype(F32)
    weight = pw_ref[...].astype(F32)
    key = lane((MC, 128)) < HD
    for f in range(4):
        total = jnp.zeros((MC, 128), F32)
        for a in range(3):
            frame = 2 * f + a - 1
            if frame < 0:
                continue
            for b in range(3):
                for g in range(3):
                    tap = 9 * a + 3 * b + g
                    total += weight[tap : tap + 1, :] * xf[b, frame, pl.ds(7 + g, MC, stride=2), :]
        mean_lo = jnp.sum(jnp.where(key, total, 0.0), axis=1, keepdims=True) / HD
        mean_hi = jnp.sum(jnp.where(key, 0.0, total), axis=1, keepdims=True) / HD
        centred = total - jnp.where(key, mean_lo, mean_hi)
        square = centred * centred
        var_lo = jnp.sum(jnp.where(key, square, 0.0), axis=1, keepdims=True) / HD
        var_hi = jnp.sum(jnp.where(key, 0.0, square), axis=1, keepdims=True) / HD
        normed = centred * lax.rsqrt(jnp.where(key, var_lo, var_hi) + 1e-06)
        fresh[f * MC : (f + 1) * MC, :] = normed.astype(BF16)

    qall[p] = qt[pl.ds(pl.multiple_of(p * HD, HD), HD), :]

    def prepare(k, i, count):
        x = kv[k][i].astype(F32)
        turned = pltpu.roll(x, HD, 1)
        low = lane((TOK, TOK)) < HD
        column = line((TOK, TOK)) % MC
        mask = jnp.where((lane((TOK, TOK)) == HD) & (column >= count), MASKED, 0.0)
        row = pl.ds(pl.multiple_of(i * TOK, TOK), TOK)
        kaug[k][row, 0:128] = jnp.where(low, x, turned).astype(BF16)
        kaug[k][row, 128:256] = jnp.where(low, x, mask).astype(BF16)
        upper = line((TOK, TOK)) < HD
        vt[k][:, row] = jnp.where(upper, 1.0, x.T).astype(BF16)

    def prepare_slot(k, count):
        def one(i, carry):
            prepare(k, i, count)
            return carry

        lax.fori_loop(0, N, one, 0, unroll=4)

    scale = HD ** (-0.5) * math.log2(math.e)
    pair0 = p // 2

    def pair_of(i):
        return lax.rem(pair0 - i + 2 * PAIRS, PAIRS)

    def block_of(i, t):
        return 2 * pair_of(2 * i + t // 2) + t % 2

    def build(b):
        x = [qall[2 * (b // 2) + j, :, pl.ds(pl.multiple_of(lax.rem(b, 2) * 128, 128), 128)] for j in range(2)]
        x = jnp.concatenate(x, axis=1).astype(F32) * scale
        first = x.astype(BF16)
        x = x - first.astype(F32)
        second = x.astype(BF16)
        x = x - second.astype(F32)
        qa[b, 0:HD, :] = first
        qa[b, HD : 2 * HD, :] = second
        qa[b, 2 * HD : 3 * HD, :] = x.astype(BF16)

    def scores(k, b, z):
        peak = None
        for c in range(0, NK[k], 128):
            block = jnp.dot(kaug[k][c : c + 128, :], qa[b], preferred_element_type=F32)
            S[z, c : c + 128, :] = block
            top = jnp.max(block.reshape(16, 8, TQ), axis=0)
            peak = top if peak is None else jnp.maximum(peak, top)
        return peak

    def weigh(k, z, peak):
        top = jnp.max(peak, axis=0, keepdims=True)
        total = None
        for c in range(0, NK[k], 256):
            weights = jnp.exp2(S[z, c : c + 256, :] - top).astype(BF16)
            part = jnp.dot(vt[k][:, c : c + 256], weights, preferred_element_type=F32)
            total = part if total is None else total + part
        return top, total

    def queries_of(pair):
        wait_bytes(qall.at[0], q_r.at[2 * pair])
        wait_bytes(qall.at[0], q_r.at[2 * pair + 1])

    kv_copy.wait()
    wait_bytes(kv0.at[pl.ds(0, N - 1)], kv_r)

    remote(kv0, kv1.at[pl.ds(0, N)], kx_s, kx_r, partner, p).start()
    for k in range(2, PAIRS):
        ask_pair(k)

    @pl.when(s != p)
    def _():
        remote(fresh, kv1.at[N], fr_s, fr_r, p, s).start()

    @pl.when(s == p)
    def _():
        kv1[N] = fresh[...]

    remote(fresh, kv1.at[N + 1], fx_s, fx_r, twin, s).start()

    prepare_slot(0, valid[s + 1])
    wait_bytes(qall.at[0], q_r.at[twin])
    queries_of(pair_of(1))
    for t in range(4):
        build(block_of(0, t))
    first_peak = scores(0, block_of(0, 0), 0)

    def own_step(i, peak):
        @pl.when((i == 3) & (s == RING - 1))
        def _():
            move_on()

        @pl.when(i < 3)
        def _():
            queries_of(pair_of(2 * i + 2))
            queries_of(pair_of(2 * i + 3))

        for t in range(4):
            b = block_of(i, t)
            build(block_of(i + 1, t))
            later = scores(0, block_of(i, t + 1) if t < 3 else block_of(i + 1, 0), (t + 1) % 2)
            top, total = weigh(0, t % 2, peak)
            st[b] = total
            sm[pl.ds(b, 1), :] = top
            peak = later
        return peak

    lax.fori_loop(0, 4, own_step, first_peak)

    wait_bytes(kv1.at[pl.ds(0, N)], kx_r)
    prepare_slot(1, valid[partner + 1])

    @pl.when(s != p)
    def _():
        wait_bytes(kv1.at[N], fr_r)

    prepare(1, N, valid[0])
    wait_bytes(kv1.at[N + 1], fx_r)
    prepare(1, N + 1, valid[0])
    def tile_of(u, k):
        return 2 * pair_of(k) + u

    def partner_step(u, i, peak):
        for t in range(4):
            b = tile_of(u, 4 * i + t)
            if t < 3:
                following = tile_of(u, 4 * i + t + 1)
            else:
                following = tile_of(jnp.minimum(u + (i + 1) // 2, 1), lax.rem(4 * i + 4, PAIRS))
            later = scores(1, following, (t + 1) % 2)
            top, total = weigh(1, t % 2, peak)
            before = sm[pl.ds(b, 1), :]
            both = jnp.maximum(top, before)
            total = total * jnp.exp2(top - both) + st[b] * jnp.exp2(before - both)
            normed = total[HD:, :] / total[:HD, :]
            lse = both + jnp.log2(total[0:1, :])
            for j in range(2):
                ot[t, j * HD : (j + 1) * HD, :] = normed[:, j * 128 : (j + 1) * 128]
                lt[u, pl.ds(b - u + j, 1), :] = lse[:, j * 128 : (j + 1) * 128]
            peak = later
        for t in range(4):
            sb[u, pair_of(4 * i + t)] = ot[t].T.astype(BF16).reshape(PAIRS, PART, 128)
        for t in range(4):
            pair = pair_of(4 * i + t)
            for d in range(1, PAIRS):
                owner = lax.rem(rank + d, PAIRS)
                remote(
                    sb.at[u, pair, owner], rb.at[u, rank, pair], res_s.at[u], res_r.at[u], 2 * owner + half, p
                ).start()
        return peak

    def tell(u):
        lse = lt[u]
        first = lse.astype(BF16).astype(F32)
        second = (lse - first).astype(BF16).astype(F32)
        third = lse - first - second
        stacked = jnp.concatenate([first, second, third, jnp.zeros((128 - 3 * N, 128), F32)], axis=0)
        ls[u] = stacked.T.astype(BF16).reshape(PAIRS, PART, 128)
        for d in range(1, PAIRS):
            owner = lax.rem(rank + d, PAIRS)
            remote(ls.at[u, owner], lr.at[u, rank], lse_s.at[u], lse_r.at[u], 2 * owner + half, p).start()
        lr[u, rank] = ls[u, rank]
        rb[u, rank] = sb[u, :, rank]

    peak = scores(1, tile_of(0, 0), 0)
    for u in range(2):
        peak = lax.fori_loop(0, 2, lambda i, peak, u=u: partner_step(u, i, peak), peak)
        tell(u)

    def combine(u):
        wait_bytes(lr.at[u, pl.ds(0, PAIRS - 1)], lse_r.at[u])
        parts = lr[u].astype(F32).reshape(PAIRS * PART, 128)
        parts = parts + pltpu.roll(parts, 128 - N, 1) + pltpu.roll(parts, 128 - 2 * N, 1)
        parts = jnp.where(lane((PAIRS * PART, 128)) < N, parts, 0.0).reshape(PAIRS, PART, 128)
        share = jnp.exp2(parts - jnp.max(parts, axis=0, keepdims=True))
        share = (share / jnp.sum(share, axis=0, keepdims=True)).reshape(PAIRS * PART, 128)
        share_hi = share.astype(BF16)
        share_lo = (share - share_hi.astype(F32)).astype(BF16)
        shares = jnp.concatenate([share_hi, share_lo], axis=1)
        wait_bytes(rb.at[u, pl.ds(0, PAIRS - 1)], res_r.at[u])
        for j in range(PAIRS):
            spread = jnp.dot(shares, sel[:, j * 128 : (j + 1) * 128], preferred_element_type=F32)
            mixed = jnp.sum(spread.reshape(PAIRS, PART, 128) * rb[u, :, j].astype(F32), axis=0)
            mx[u, j] = mixed.astype(BF16)

        for d in range(1, N):
            peer = lax.rem(p + d, N)
            remote(mx.at[u, peer // 2], mr.at[u, 0, p], mx_s.at[u], mx_r.at[u], s, peer).start()
        for d in range(N):
            peer = lax.rem(p + d, N)
            remote(mx.at[u, peer // 2], mr.at[u, 1, p], my_s.at[u], my_r.at[u], across, peer).start()
        mr[u, 0, p] = mx[u, p // 2]

    def project(u):
        wait_bytes(mr.at[u, 0, pl.ds(0, N - 1)], mx_r.at[u])
        wait_bytes(mr.at[u, 1], my_r.at[u])
        odd = lax.rem(p, 2) == 1
        left = lane((2 * PART, 128)) < HD
        pieces = []
        for j in range(PAIRS):
            a = mr[u, :, 2 * j].astype(F32).reshape(2 * PART, 128)
            b = mr[u, :, 2 * j + 1].astype(F32).reshape(2 * PART, 128)
            a = jnp.where(odd, pltpu.roll(a, HD, 1), a)
            b = jnp.where(odd, b, pltpu.roll(b, HD, 1))
            pieces.append(jnp.where(left, a, b).astype(BF16))
        heads = jnp.concatenate(pieces, axis=1)
        att[u] = jnp.dot(heads, wv[...], preferred_element_type=F32).astype(BF16)


    def start_of(index, c):
        return pl.multiple_of(lax.rem(index, 2) * TQ + c * 128 + index // 2 * PART, PART)

    def rows(index, c):
        return out.at[pl.ds(start_of(index, c), PART), :]

    def near(dz):
        return y * RING + lax.rem(z + dz + RING, RING)

    def far(dz):
        return (1 - y) * RING + lax.rem(z + dz + RING, RING)

    sent = [0]

    def push(index, target, c, src=None):
        remote(
            rows(index, c) if src is None else src, rows(index, c), at_s.at[sent[0]], at_r.at[CUT * index + c], target, p
        ).start()
        sent[0] += 1

    def got(index, c):
        wait_bytes(rows(0, 0), at_r.at[CUT * index + c])

    def begin(c):
        for i, index in enumerate((s, across)):
            piece = slice(i * PART, (i + 1) * PART)
            push(index, near(1), c, att.at[c, piece, :])
            push(index, near(-1), c, att.at[c, piece, :])
            out[pl.ds(start_of(index, c), PART), :] = att[c, piece, :]

    def pass_near(k, c):
        got(near(-k), c)
        if k < 4:
            push(near(-k), near(1), c)
            got(near(k), c)
        if k < 3:
            push(near(k), near(-1), c)

    def pass_far_on(k, c):
        got(far(k), c)
        if k < 4:
            push(far(k), near(-1), c)
            got(far(-k), c)
        if k < 3:
            push(far(-k), near(1), c)

    def go_round(k, c):
        pass_near(k, c)
        pass_far_on(k, c)

    combine(0)
    combine(1)
    w_copy.wait()
    project(0)
    begin(0)
    go_round(1, 0)
    go_round(2, 0)
    project(1)
    begin(1)
    go_round(1, 1)
    go_round(3, 0)
    go_round(2, 1)
    go_round(4, 0)
    go_round(3, 1)
    go_round(4, 1)

    for i in range(sent[0]):
        wait_bytes(rows(0, 0), at_s.at[i])
    wait_bytes(kv0.at[pl.ds(0, N - 1)], kv_s)
    wait_bytes(kv1.at[pl.ds(0, N)], kx_s)
    wait_bytes(qall.at[pl.ds(0, N - 1)], q_s)
    for u in range(2):
        wait_bytes(rb.at[u, pl.ds(0, PAIRS - 1)], res_s.at[u])
        wait_bytes(lr.at[u, pl.ds(0, PAIRS - 1)], lse_s.at[u])
        wait_bytes(mr.at[u, 0, pl.ds(0, N - 1)], mx_s.at[u])
        wait_bytes(mr.at[u, 1], my_s.at[u])
    wait_bytes(kv1.at[N + 1], fx_s)

    @pl.when(p < N - 1)
    def _():
        wait_bytes(halo, halo_s)

    @pl.when(s != p)
    def _():
        wait_bytes(kv1.at[N], fr_s)

    @pl.when(s < N - 1)
    def _():
        wait_bytes(old_hbm, ag_s)

    @pl.when(s > 0)
    def _():
        wait_bytes(old_hbm, ag_r)

    @pl.when(s == 0)
    def _():
        pltpu.make_async_copy(zeros, aged, lsem5).wait()


def settle(a, b, c, a_out, b_out, c_out, a_mid, b_mid, c_mid, ins, outs):
    moves = []
    for src, mid, dst, parts in zip((a, c, b), (a_mid, c_mid, b_mid), (a_out, c_out, b_out), (4, 2, 1)):
        rows = src.shape[0] // parts
        for i in range(parts):
            part = pl.ds(i * rows, rows)
            n = len(moves)
            moves.append(
                (
                    pltpu.make_async_copy(src.at[part, :], mid.at[part, :], ins.at[n]),
                    pltpu.make_async_copy(mid.at[part, :], dst.at[part, :], outs.at[n]),
                )
            )
    for first, _ in moves:
        first.start()
    for first, second in moves:
        first.wait()
        second.start()
    for _, second in moves:
        second.wait()


def local(queries, raw_clip, pool_weight, old_memory, valid_columns, out_weight):
    dma = pltpu.SemaphoreType.DMA
    anywhere = pl.BlockSpec(memory_space=pl.ANY)
    vmem = pl.BlockSpec(memory_space=pltpu.VMEM)
    attended, fresh, aged = pl.pallas_call(
        kernel,
        out_shape=(
            jax.ShapeDtypeStruct((QB, N * HD), BF16),
            jax.ShapeDtypeStruct((TOK, TOK), BF16),
            jax.ShapeDtypeStruct((TOK, N * TOK), BF16),
        ),
        in_specs=[anywhere, anywhere, vmem, anywhere, pl.BlockSpec(memory_space=pltpu.SMEM), anywhere],
        out_specs=(vmem, vmem, anywhere),
        scratch_shapes=[
            pltpu.VMEM((TQ, N * HD), BF16),
            pltpu.VMEM((N * HD, TQ), BF16),
            pltpu.VMEM((N, HD, TQ), BF16),
            pltpu.VMEM((N, TOK, TOK), BF16),
            pltpu.VMEM((N + 2, TOK, TOK), BF16),
            pltpu.VMEM((NK[0], 256), BF16),
            pltpu.VMEM((NK[1], 256), BF16),
            pltpu.VMEM((128, NK[0]), BF16),
            pltpu.VMEM((128, NK[1]), BF16),
            pltpu.VMEM((2, NK[1], TQ), F32),
            pltpu.VMEM((N, 256, TQ), BF16),
            pltpu.VMEM((N, 128, TQ), F32),
            pltpu.VMEM((N, TQ), F32),
            pltpu.VMEM((4, 128, 128), F32),
            pltpu.VMEM((2, N, 128), F32),
            pltpu.VMEM((2, PAIRS, PAIRS, PART, 128), BF16),
            pltpu.VMEM((2, PAIRS, PAIRS, PART, 128), BF16),
            pltpu.VMEM((2, PAIRS, PART, 128), BF16),
            pltpu.VMEM((2, PAIRS, PART, 128), BF16),
            pltpu.VMEM((2, PAIRS, PART, 128), BF16),
            pltpu.VMEM((2, 2, N, PART, 128), BF16),
            pltpu.VMEM((2, 2 * PART, N * HD), BF16),
            pltpu.VMEM((256, N * HD), BF16),
            pltpu.VMEM((N * HD, N * HD), BF16),
            pltpu.VMEM((8, 2, 64, 128), BF16),
            pltpu.VMEM((8, 64, 128), BF16),
            pltpu.VMEM((3, 8, 72, 128), F32),
            pltpu.VMEM((TOK, N * TOK), BF16),
            *[dma] * 5,
            *[dma] * 7,
            dma((N,)),
            *[dma] * 6,
            *[dma((2,))] * 8,
            dma((N * CUT,)),
            dma((N * CUT,)),
        ],
        compiler_params=pltpu.CompilerParams(
            collective_id=0, has_side_effects=True, vmem_limit_bytes=60 * 1024 * 1024
        ),
        name="attend",
    )(
        queries,
        raw_clip,
        pool_weight,
        old_memory.reshape(TOK, N * TOK),
        valid_columns,
        out_weight,
    )
    shapes = tuple(jax.ShapeDtypeStruct(x.shape, x.dtype) for x in (attended, fresh, aged))
    attended, fresh, aged = pl.pallas_call(
        settle,
        out_shape=shapes,
        in_specs=[anywhere] * 3,
        out_specs=(anywhere,) * 3,
        scratch_shapes=[*(pltpu.VMEM(x.shape, x.dtype) for x in shapes), dma((7,)), dma((7,))],
        compiler_params=pltpu.CompilerParams(vmem_limit_bytes=60 * 1024 * 1024),
        name="settle",
    )(attended, fresh, aged)
    return (attended, fresh.reshape(4, 1, MC, TOK), aged.reshape(old_memory.shape))


def solution(mesh):
    return jax.shard_map(
        local,
        mesh=mesh,
        in_specs=(
            P("space", None),
            P(None, "space", None, "slot"),
            P(None, "slot"),
            P("slot", None, "space", None, None),
            P(),
            P(),
        ),
        out_specs=(
            P("space", None),
            P(None, "space", None, "slot"),
            P("slot", None, "space", None, None),
        ),
        check_vma=False,
    )
```

```python
import math

import jax
import jax.numpy as jnp
from jax import lax
from jax.experimental import pallas as pl
from jax.experimental.pallas import tpu as pltpu
from jax.sharding import PartitionSpec as P

F32 = jnp.float32
BF16 = jnp.bfloat16
MESH = pl.DeviceIdType.MESH
N = 16
HD = 64
TOK = 128
QB = 512
NK = (N * TOK, (N + 2) * TOK)
TQ = 256
MC = 32
MASKED = -1e30
PAIRS = N // 2
OWN = QB // N
RING = 8
CUT = 2


def to(slot, space):
    return {"slot": slot, "space": space}


def remote(src, dst, send, recv, slot, space):
    return pltpu.make_async_remote_copy(
        src_ref=src, dst_ref=dst, send_sem=send, recv_sem=recv, device_id=to(slot, space), device_id_type=MESH
    )


def wait_bytes(ref, sem):
    pltpu.make_async_copy(ref, ref, sem).wait()


def kernel(
    q_hbm, raw_hbm, pw_ref, old_hbm, valid, w_hbm,
    out, fresh, aged,
    qv, qt, qall, kv0, kv1, kaug0, kaug1, vt0, vt1, S, qa, st, sm, ot, lt, sb, rb, ls, lr, mx, mr, att, sel, wv, rawv, halo, xf, zeros,
    lsem, lsem2, lsem3, lsem4, lsem5,
    halo_s, halo_r, kv_s, kv_r, kx_s, kx_r, q_s, q_r, fr_s, fr_r, fx_s, fx_r, ag_s, ag_r,
    res_s, res_r, lse_s, lse_r, mx_s, mx_r, my_s, my_r, at_s, at_r,
):
    s = lax.axis_index("slot")
    p = lax.axis_index("space")
    half = lax.rem(s, 2)
    rank = s // 2
    partner = s + 1 - 2 * half
    twin = p + 1 - 2 * lax.rem(p, 2)
    y, z = s // RING, lax.rem(s, RING)
    across = lax.rem(s + RING, N)
    kv, kaug, vt = (kv0, kv1), (kaug0, kaug1), (vt0, vt1)
    lane = lambda shape: lax.broadcasted_iota(jnp.int32, shape, 1)
    line = lambda shape: lax.broadcasted_iota(jnp.int32, shape, 0)

    def head_of(index):
        return old_hbm.at[:, pl.ds(pl.multiple_of(index * TOK, TOK), TOK)]

    q_copy = pltpu.make_async_copy(q_hbm.at[pl.ds(pl.multiple_of(half * TQ, TQ), TQ), :], qv, lsem)
    q_copy.start()
    raw_copy = pltpu.make_async_copy(raw_hbm, rawv, lsem2)
    raw_copy.start()
    kv_copy = pltpu.make_async_copy(head_of(p), kv0.at[p], lsem3)
    kv_copy.start()
    w_copy = pltpu.make_async_copy(w_hbm, wv, lsem4)
    w_copy.start()

    barrier = pltpu.get_barrier_semaphore()

    def greet(slot, space):
        pl.semaphore_signal(barrier, inc=1, device_id=to(slot, space), device_id_type=MESH)

    for d in range(1, N):
        greet(s, lax.rem(p + d, N))
    for d in range(1, N):
        greet(across, lax.rem(p + d, N))
    for d in range(1, N):
        greet(lax.rem(s + d, N), p)
    greet(twin, s)
    greet(p, partner)

    @pl.when(s != p)
    def _():
        greet(p, s)

    q_copy.wait()
    for c in range(PAIRS):
        qt[c * 128 : (c + 1) * 128, :] = qv[:, c * 128 : (c + 1) * 128].T

    row_i = line((256, N * HD))
    col_i = lane((256, N * HD))
    sel[...] = jnp.where(row_i % 128 == col_i // HD, 1.0, 0.0).astype(BF16)
    ones_row = jnp.where(line((HD, TQ)) == 0, 1.0, 0.0).astype(BF16)
    for b in range(N):
        qa[b, 3 * HD :, :] = ones_row

    @pl.when(s != p)
    def _():
        pl.semaphore_wait(barrier, 3 * (N - 1) + 3)

    @pl.when(s == p)
    def _():
        pl.semaphore_wait(barrier, 3 * (N - 1) + 2)

    @pl.when(p < N - 1)
    def _():
        remote(raw_hbm.at[:, 1], halo, halo_s, halo_r, s, p + 1).start()

    for d in range(1, N):
        peer = lax.rem(p + d, N)
        remote(head_of(peer), kv0.at[p], kv_s, kv_r, s, peer).start()

    def ask(peer):
        remote(qt.at[pl.ds(pl.multiple_of(peer * HD, HD), HD), :], qall.at[p], q_s, q_r.at[p], s, peer).start()

    def ask_pair(k):
        for b in range(2):
            ask(2 * lax.rem(p // 2 + k, PAIRS) + b)

    ask(twin)
    ask_pair(1)

    def move_on():
        remote(old_hbm, aged, ag_s, ag_r, s + 1, p).start()

    @pl.when((s != RING - 1) & (s < N - 1))
    def _():
        move_on()

    @pl.when(s == 0)
    def _():
        zeros[...] = jnp.zeros_like(zeros)
        pltpu.make_async_copy(zeros, aged, lsem5).start()

    raw_copy.wait()

    @pl.when(p > 0)
    def _():
        wait_bytes(halo, halo_r)

    @pl.when(p == 0)
    def _():
        halo[...] = jnp.zeros_like(halo)

    edge = jnp.zeros((8, 8, 128), F32)
    for b in range(3):
        xf[b, :, 0:8, :] = edge
        xf[b, :, 8:, :] = (halo[...] if b == 0 else rawv[:, b - 1]).astype(F32)
    weight = pw_ref[...].astype(F32)
    key = lane((MC, 128)) < HD
    for f in range(4):
        total = jnp.zeros((MC, 128), F32)
        for a in range(3):
            frame = 2 * f + a - 1
            if frame < 0:
                continue
            for b in range(3):
                for g in range(3):
                    tap = 9 * a + 3 * b + g
                    total += weight[tap : tap + 1, :] * xf[b, frame, pl.ds(7 + g, MC, stride=2), :]
        mean_lo = jnp.sum(jnp.where(key, total, 0.0), axis=1, keepdims=True) / HD
        mean_hi = jnp.sum(jnp.where(key, 0.0, total), axis=1, keepdims=True) / HD
        centred = total - jnp.where(key, mean_lo, mean_hi)
        square = centred * centred
        var_lo = jnp.sum(jnp.where(key, square, 0.0), axis=1, keepdims=True) / HD
        var_hi = jnp.sum(jnp.where(key, 0.0, square), axis=1, keepdims=True) / HD
        normed = centred * lax.rsqrt(jnp.where(key, var_lo, var_hi) + 1e-06)
        fresh[f * MC : (f + 1) * MC, :] = normed.astype(BF16)

    qall[p] = qt[pl.ds(pl.multiple_of(p * HD, HD), HD), :]

    def prepare(k, i, count):
        x = kv[k][i].astype(F32)
        turned = pltpu.roll(x, HD, 1)
        low = lane((TOK, TOK)) < HD
        column = line((TOK, TOK)) % MC
        mask = jnp.where((lane((TOK, TOK)) == HD) & (column >= count), MASKED, 0.0)
        row = pl.ds(pl.multiple_of(i * TOK, TOK), TOK)
        kaug[k][row, 0:128] = jnp.where(low, x, turned).astype(BF16)
        kaug[k][row, 128:256] = jnp.where(low, x, mask).astype(BF16)
        upper = line((TOK, TOK)) < HD
        vt[k][:, row] = jnp.where(upper, 1.0, x.T).astype(BF16)

    def prepare_slot(k, count):
        def one(i, carry):
            prepare(k, i, count)
            return carry

        lax.fori_loop(0, N, one, 0, unroll=4)

    scale = HD ** (-0.5) * math.log2(math.e)
    pair0 = p // 2

    def pair_of(i):
        return lax.rem(pair0 - i + 2 * PAIRS, PAIRS)

    def block_of(i, t):
        return 2 * pair_of(2 * i + t // 2) + t % 2

    def build(b):
        x = qall[b].astype(F32) * scale
        first = x.astype(BF16)
        x = x - first.astype(F32)
        second = x.astype(BF16)
        x = x - second.astype(F32)
        qa[b, 0:HD, :] = first
        qa[b, HD : 2 * HD, :] = second
        qa[b, 2 * HD : 3 * HD, :] = x.astype(BF16)

    def scores(k, b, z):
        peak = None
        for c in range(0, NK[k], 128):
            block = jnp.dot(kaug[k][c : c + 128, :], qa[b], preferred_element_type=F32)
            S[z, c : c + 128, :] = block
            top = jnp.max(block.reshape(16, 8, TQ), axis=0)
            peak = top if peak is None else jnp.maximum(peak, top)
        return peak

    def weigh(k, z, peak):
        top = jnp.max(peak, axis=0, keepdims=True)
        total = None
        for c in range(0, NK[k], 256):
            weights = jnp.exp2(S[z, c : c + 256, :] - top).astype(BF16)
            part = jnp.dot(vt[k][:, c : c + 256], weights, preferred_element_type=F32)
            total = part if total is None else total + part
        return top, total

    def queries_of(pair):
        wait_bytes(qall.at[0], q_r.at[2 * pair])
        wait_bytes(qall.at[0], q_r.at[2 * pair + 1])

    kv_copy.wait()
    wait_bytes(kv0.at[pl.ds(0, N - 1)], kv_r)

    remote(kv0, kv1.at[pl.ds(0, N)], kx_s, kx_r, partner, p).start()
    for k in range(2, PAIRS):
        ask_pair(k)

    @pl.when(s != p)
    def _():
        remote(fresh, kv1.at[N], fr_s, fr_r, p, s).start()

    @pl.when(s == p)
    def _():
        kv1[N] = fresh[...]

    remote(fresh, kv1.at[N + 1], fx_s, fx_r, twin, s).start()

    prepare_slot(0, valid[s + 1])
    wait_bytes(qall.at[0], q_r.at[twin])
    queries_of(pair_of(1))
    for t in range(4):
        build(block_of(0, t))
    first_peak = scores(0, block_of(0, 0), 0)

    def own_step(i, peak):
        @pl.when((i == 1) & (s == RING - 1))
        def _():
            move_on()

        @pl.when(i < 3)
        def _():
            queries_of(pair_of(2 * i + 2))
            queries_of(pair_of(2 * i + 3))

        for t in range(4):
            b = block_of(i, t)
            build(block_of(i + 1, t))
            later = scores(0, block_of(i, t + 1) if t < 3 else block_of(i + 1, 0), (t + 1) % 2)
            top, total = weigh(0, t % 2, peak)
            st[b] = total
            sm[pl.ds(b, 1), :] = top
            peak = later
        return peak

    lax.fori_loop(0, 4, own_step, first_peak)

    wait_bytes(kv1.at[pl.ds(0, N)], kx_r)
    prepare_slot(1, valid[partner + 1])

    @pl.when(s != p)
    def _():
        wait_bytes(kv1.at[N], fr_r)

    prepare(1, N, valid[0])
    wait_bytes(kv1.at[N + 1], fx_r)
    prepare(1, N + 1, valid[0])
    first_peak = scores(1, block_of(0, 0), 0)

    def partner_step(i, peak):
        for t in range(4):
            b = block_of(i, t)
            later = scores(1, block_of(i, t + 1) if t < 3 else block_of(i + 1, 0), (t + 1) % 2)
            top, total = weigh(1, t % 2, peak)
            before = sm[pl.ds(b, 1), :]
            both = jnp.maximum(top, before)
            total = total * jnp.exp2(top - both) + st[b] * jnp.exp2(before - both)
            ot[t // 2, (t % 2) * HD : (t % 2 + 1) * HD, :] = total[HD:, :] / total[:HD, :]
            lt[pl.ds(b, 1), :] = both + jnp.log2(total[0:1, :])
            peak = later
        for u in range(2):
            sb[pair_of(2 * i + u)] = ot[u].T.astype(BF16).reshape(PAIRS, OWN, 128)
        for u in range(2):
            pair = pair_of(2 * i + u)
            for d in range(1, PAIRS):
                owner = lax.rem(rank + d, PAIRS)
                remote(sb.at[pair, owner], rb.at[rank, pair], res_s, res_r, 2 * owner + half, p).start()
        return peak

    lax.fori_loop(0, 4, partner_step, first_peak)

    lse = lt[...]
    first = lse.astype(BF16).astype(F32)
    second = (lse - first).astype(BF16).astype(F32)
    third = lse - first - second
    stacked = jnp.concatenate([first, second, third, jnp.zeros((128 - 3 * N, TQ), F32)], axis=0)
    ls[...] = stacked.T.astype(BF16).reshape(PAIRS, OWN, 128)
    for d in range(1, PAIRS):
        owner = lax.rem(rank + d, PAIRS)
        remote(ls.at[owner], lr.at[rank], lse_s, lse_r, 2 * owner + half, p).start()
    lr[rank] = ls[rank]
    rb[rank] = sb[:, rank]

    wait_bytes(lr.at[pl.ds(0, PAIRS - 1)], lse_r)
    parts = lr[...].astype(F32).reshape(PAIRS * OWN, 128)
    parts = parts + pltpu.roll(parts, 128 - N, 1) + pltpu.roll(parts, 128 - 2 * N, 1)
    parts = jnp.where(lane((PAIRS * OWN, 128)) < N, parts, 0.0).reshape(PAIRS, OWN, 128)
    share = jnp.exp2(parts - jnp.max(parts, axis=0, keepdims=True))
    share = (share / jnp.sum(share, axis=0, keepdims=True)).reshape(PAIRS * OWN, 128)
    share_hi = share.astype(BF16)
    share_lo = (share - share_hi.astype(F32)).astype(BF16)
    shares = jnp.concatenate([share_hi, share_lo], axis=1)
    wait_bytes(rb.at[pl.ds(0, PAIRS - 1)], res_r)
    for j in range(PAIRS):
        spread = jnp.dot(shares, sel[:, j * 128 : (j + 1) * 128], preferred_element_type=F32)
        mixed = jnp.sum(spread.reshape(PAIRS, OWN, 128) * rb[:, j].astype(F32), axis=0)
        mx[j] = mixed.astype(BF16)

    for d in range(1, N):
        peer = lax.rem(p + d, N)
        remote(mx.at[peer // 2], mr.at[0, p], mx_s, mx_r, s, peer).start()
    for d in range(N):
        peer = lax.rem(p + d, N)
        remote(mx.at[peer // 2], mr.at[1, p], my_s, my_r, across, peer).start()
    mr[0, p] = mx[p // 2]
    w_copy.wait()
    wait_bytes(mr.at[0, pl.ds(0, N - 1)], mx_r)
    wait_bytes(mr.at[1], my_r)
    odd = lax.rem(p, 2) == 1
    left = lane((2 * OWN, 128)) < HD
    pieces = []
    for j in range(PAIRS):
        a = mr[:, 2 * j].astype(F32).reshape(2 * OWN, 128)
        b = mr[:, 2 * j + 1].astype(F32).reshape(2 * OWN, 128)
        a = jnp.where(odd, pltpu.roll(a, HD, 1), a)
        b = jnp.where(odd, b, pltpu.roll(b, HD, 1))
        pieces.append(jnp.where(left, a, b).astype(BF16))
    heads = jnp.concatenate(pieces, axis=1)
    att[...] = jnp.dot(heads, wv[...], preferred_element_type=F32).astype(BF16)

    PART = OWN // CUT

    def start_of(index, c):
        return pl.multiple_of((lax.rem(index, 2) * PAIRS + index // 2) * OWN + c * PART, PART)

    def rows(index, c):
        return out.at[pl.ds(start_of(index, c), PART), :]

    def near(dz):
        return y * RING + lax.rem(z + dz + RING, RING)

    def far(dz):
        return (1 - y) * RING + lax.rem(z + dz + RING, RING)

    sent = [0]

    def push(index, target, c, src=None):
        remote(
            rows(index, c) if src is None else src, rows(index, c), at_s.at[sent[0]], at_r.at[CUT * index + c], target, p
        ).start()
        sent[0] += 1

    def got(index, c):
        wait_bytes(rows(0, 0), at_r.at[CUT * index + c])

    for c in range(CUT):
        for i, index in enumerate((s, across)):
            piece = slice(i * OWN + c * PART, i * OWN + (c + 1) * PART)
            push(index, near(1), c, att.at[piece, :])
            push(index, near(-1), c, att.at[piece, :])
            out[pl.ds(start_of(index, c), PART), :] = att[piece, :]

    def pass_near(k, c):
        got(near(-k), c)
        if k < 4:
            push(near(-k), near(1), c)
            got(near(k), c)
        if k < 3:
            push(near(k), near(-1), c)

    def pass_far_on(k, c):
        got(far(k), c)
        if k < 4:
            push(far(k), near(-1), c)
            got(far(-k), c)
        if k < 3:
            push(far(-k), near(1), c)

    for k in range(1, 5):
        for c in range(CUT):
            pass_near(k, c)
            pass_far_on(k, c)

    for i in range(sent[0]):
        wait_bytes(rows(0, 0), at_s.at[i])
    wait_bytes(kv0.at[pl.ds(0, N - 1)], kv_s)
    wait_bytes(kv1.at[pl.ds(0, N)], kx_s)
    wait_bytes(qall.at[pl.ds(0, N - 1)], q_s)
    wait_bytes(rb.at[pl.ds(0, PAIRS - 1)], res_s)
    wait_bytes(lr.at[pl.ds(0, PAIRS - 1)], lse_s)
    wait_bytes(mr.at[0, pl.ds(0, N - 1)], mx_s)
    wait_bytes(mr.at[1], my_s)
    wait_bytes(kv1.at[N + 1], fx_s)

    @pl.when(p < N - 1)
    def _():
        wait_bytes(halo, halo_s)

    @pl.when(s != p)
    def _():
        wait_bytes(kv1.at[N], fr_s)

    @pl.when(s < N - 1)
    def _():
        wait_bytes(old_hbm, ag_s)

    @pl.when(s > 0)
    def _():
        wait_bytes(old_hbm, ag_r)

    @pl.when(s == 0)
    def _():
        pltpu.make_async_copy(zeros, aged, lsem5).wait()


def settle(a, b, c, a_out, b_out, c_out, a_mid, b_mid, c_mid, ins, outs):
    moves = []
    for src, mid, dst, parts in zip((a, c, b), (a_mid, c_mid, b_mid), (a_out, c_out, b_out), (4, 2, 1)):
        rows = src.shape[0] // parts
        for i in range(parts):
            part = pl.ds(i * rows, rows)
            n = len(moves)
            moves.append(
                (
                    pltpu.make_async_copy(src.at[part, :], mid.at[part, :], ins.at[n]),
                    pltpu.make_async_copy(mid.at[part, :], dst.at[part, :], outs.at[n]),
                )
            )
    for first, _ in moves:
        first.start()
    for first, second in moves:
        first.wait()
        second.start()
    for _, second in moves:
        second.wait()


def local(queries, raw_clip, pool_weight, old_memory, valid_columns, out_weight):
    dma = pltpu.SemaphoreType.DMA
    anywhere = pl.BlockSpec(memory_space=pl.ANY)
    vmem = pl.BlockSpec(memory_space=pltpu.VMEM)
    attended, fresh, aged = pl.pallas_call(
        kernel,
        out_shape=(
            jax.ShapeDtypeStruct((QB, N * HD), BF16),
            jax.ShapeDtypeStruct((TOK, TOK), BF16),
            jax.ShapeDtypeStruct((TOK, N * TOK), BF16),
        ),
        in_specs=[anywhere, anywhere, vmem, anywhere, pl.BlockSpec(memory_space=pltpu.SMEM), anywhere],
        out_specs=(vmem, vmem, anywhere),
        scratch_shapes=[
            pltpu.VMEM((TQ, N * HD), BF16),
            pltpu.VMEM((N * HD, TQ), BF16),
            pltpu.VMEM((N, HD, TQ), BF16),
            pltpu.VMEM((N, TOK, TOK), BF16),
            pltpu.VMEM((N + 2, TOK, TOK), BF16),
            pltpu.VMEM((NK[0], 256), BF16),
            pltpu.VMEM((NK[1], 256), BF16),
            pltpu.VMEM((128, NK[0]), BF16),
            pltpu.VMEM((128, NK[1]), BF16),
            pltpu.VMEM((2, NK[1], TQ), F32),
            pltpu.VMEM((N, 256, TQ), BF16),
            pltpu.VMEM((N, 128, TQ), F32),
            pltpu.VMEM((N, TQ), F32),
            pltpu.VMEM((2, 128, TQ), F32),
            pltpu.VMEM((N, TQ), F32),
            pltpu.VMEM((PAIRS, PAIRS, OWN, 128), BF16),
            pltpu.VMEM((PAIRS, PAIRS, OWN, 128), BF16),
            pltpu.VMEM((PAIRS, OWN, 128), BF16),
            pltpu.VMEM((PAIRS, OWN, 128), BF16),
            pltpu.VMEM((PAIRS, OWN, 128), BF16),
            pltpu.VMEM((2, N, OWN, 128), BF16),
            pltpu.VMEM((2 * OWN, N * HD), BF16),
            pltpu.VMEM((256, N * HD), BF16),
            pltpu.VMEM((N * HD, N * HD), BF16),
            pltpu.VMEM((8, 2, 64, 128), BF16),
            pltpu.VMEM((8, 64, 128), BF16),
            pltpu.VMEM((3, 8, 72, 128), F32),
            pltpu.VMEM((TOK, N * TOK), BF16),
            *[dma] * 5,
            *[dma] * 7,
            dma((N,)),
            *[dma] * 14,
            dma((N * CUT,)),
            dma((N * CUT,)),
        ],
        compiler_params=pltpu.CompilerParams(
            collective_id=0, has_side_effects=True, vmem_limit_bytes=60 * 1024 * 1024
        ),
        name="attend",
    )(
        queries,
        raw_clip,
        pool_weight,
        old_memory.reshape(TOK, N * TOK),
        valid_columns,
        out_weight,
    )
    shapes = tuple(jax.ShapeDtypeStruct(x.shape, x.dtype) for x in (attended, fresh, aged))
    attended, fresh, aged = pl.pallas_call(
        settle,
        out_shape=shapes,
        in_specs=[anywhere] * 3,
        out_specs=(anywhere,) * 3,
        scratch_shapes=[*(pltpu.VMEM(x.shape, x.dtype) for x in shapes), dma((7,)), dma((7,))],
        compiler_params=pltpu.CompilerParams(vmem_limit_bytes=60 * 1024 * 1024),
        name="settle",
    )(attended, fresh, aged)
    return (attended, fresh.reshape(4, 1, MC, TOK), aged.reshape(old_memory.shape))


def solution(mesh):
    return jax.shard_map(
        local,
        mesh=mesh,
        in_specs=(
            P("space", None),
            P(None, "space", None, "slot"),
            P(None, "slot"),
            P("slot", None, "space", None, None),
            P(),
            P(),
        ),
        out_specs=(
            P("space", None),
            P(None, "space", None, "slot"),
            P("slot", None, "space", None, None),
        ),
        check_vma=False,
    )
```
